128 devices in a mesh: seq: 32 (over z, y_hi, x), grp: 4 (over y_lo, core).
Axes of the slice: x: 4, y: 4 (y_hi: 2, y_lo: 2; y = y_hi * 2 + y_lo), z: 4, core: 2. Of those that a mesh axis runs over, the one named last changes fastest.
Arguments:
- query_vecs: bfloat16 [65536, 1024], P(('seq', 'grp')), may hold values from -6 to 6
- key_vecs: bfloat16 [65536, 1024], P(('seq', 'grp')), may hold values from -6 to 6
- value_vecs: bfloat16 [65536, 1024], P(('seq', 'grp')), may hold values from -6 to 6
Outputs:
- attended: bfloat16 [65536, 1024], P(('seq', 'grp'))
The draws below stay inside these ranges and needn't reach their ends.
All inputs are finite; a program needn't handle non-finite values.
Results may differ from the reference program's by a relative error of at most 0.0033.
Values may be sent and summed in bfloat16 or wider, within the bound.
A program may use at most 128 MiB of HBM per device.

```python
import math
import jax
import jax.numpy as jnp
from jax import lax

HEADS = 8
HEAD_DIM = 128
BLK = 256
LEV = 4
TOKENS = 65536


def smooth_part(key, col_count):
    periods = jax.random.randint(jax.random.fold_in(key, 1), (col_count,), 4 * BLK, 64 * BLK)
    shifts = jax.random.randint(jax.random.fold_in(key, 2), (col_count,), 0, 64 * BLK)
    amplitude = jax.random.uniform(jax.random.fold_in(key, 3), (col_count,), jnp.float32, 0.5, 1.0)
    places = jnp.arange(TOKENS, dtype=jnp.int32)[:, None]
    phase = ((places + shifts[None, :]) % periods[None, :]).astype(jnp.float32) / periods[None, :].astype(jnp.float32)
    return amplitude[None, :] * jnp.sin(2.0 * math.pi * phase)


def rough_part(key, col_count):
    return jax.random.normal(key, (TOKENS, col_count), jnp.float32)


def draw_query_vecs(key, part):
    col_count = HEADS * HEAD_DIM
    base = jax.random.fold_in(key, 101)
    mixed = 0.8 * rough_part(jax.random.fold_in(base, 0), col_count) + 0.6 * smooth_part(jax.random.fold_in(base, 5), col_count)
    return jnp.clip(mixed, -6.0, 6.0).astype(jnp.bfloat16)


def draw_key_vecs(key, part):
    col_count = HEADS * HEAD_DIM
    base = jax.random.fold_in(key, 202)
    mixed = 0.8 * rough_part(jax.random.fold_in(base, 0), col_count) + 0.6 * smooth_part(jax.random.fold_in(base, 5), col_count)
    return jnp.clip(mixed, -6.0, 6.0).astype(jnp.bfloat16)


def draw_value_vecs(key, part):
    col_count = HEADS * HEAD_DIM
    base = jax.random.fold_in(key, 303)
    mixed = rough_part(jax.random.fold_in(base, 0), col_count) + 0.8 * smooth_part(jax.random.fold_in(base, 5), col_count)
    return jnp.clip(mixed, -6.0, 6.0).astype(jnp.bfloat16)


def setup_inputs(seed: int = 0) -> dict:
    key_of = jax.random.split(jax.random.key(seed), 4)
    return {
        "query_vecs": draw_query_vecs(jax.random.fold_in(key_of[3], 71), 0),
        "key_vecs": draw_key_vecs(jax.random.fold_in(key_of[3], 71), 0),
        "value_vecs": draw_value_vecs(jax.random.fold_in(key_of[3], 71), 0),
    }


very_negative = -1e+30

def coarsen_rows(rows_in, factor):
    row_count, col_count = rows_in.shape
    paired = rows_in.reshape(row_count // 2, 2, col_count).astype(jnp.float32)
    return lax.optimization_barrier(((paired[:, 0] + paired[:, 1]) * factor).astype(jnp.bfloat16))

def attend_level(queries, keys_pad, values_pad, height, head_size, first_block, block_total, block_rows):
    row_count, col_count = queries.shape
    head_count = col_count // head_size
    block_count = row_count // block_rows
    group_size = min(block_count, max(1, 512 // block_rows))
    step_count = block_count // group_size
    if height == 0:
        offsets = (0, 1, 2)
    else:
        offsets = (0, 2)
    window = len(offsets) * block_rows
    score_scale = 1.0 / math.sqrt(head_size)
    query_place = jnp.arange(block_rows, dtype=jnp.int32)
    key_place = jnp.arange(window, dtype=jnp.int32)
    key_side = key_place // block_rows
    key_upper = key_place % block_rows >= block_rows // 2
    query_upper = query_place >= block_rows // 2
    below = jnp.logical_and(jnp.logical_not(query_upper)[:, None], key_upper[None, :])
    above = jnp.logical_and(query_upper[:, None], jnp.logical_not(key_upper)[None, :])
    excluded = jnp.where(key_side[None, :] == 0, below, above)
    if height == 0:
        excluded = jnp.zeros_like(excluded)
    shifts = jnp.array([offset - 1 for offset in offsets], dtype=jnp.int32)
    other_shift = jnp.repeat(shifts, block_rows)

    def one_group(group_index):
        start = group_index * group_size * block_rows
        query_blk = lax.dynamic_slice_in_dim(queries, start, group_size * block_rows, 0).reshape(group_size, block_rows, head_count, head_size)
        key_blk = lax.dynamic_slice_in_dim(keys_pad, start, (group_size + 2) * block_rows, 0).reshape(group_size + 2, block_rows, head_count, head_size)
        value_blk = lax.dynamic_slice_in_dim(values_pad, start, (group_size + 2) * block_rows, 0).reshape(group_size + 2, block_rows, head_count, head_size)
        key_win = jnp.concatenate([key_blk[offset:offset + group_size] for offset in offsets], axis=1)
        value_win = jnp.concatenate([value_blk[offset:offset + group_size] for offset in offsets], axis=1)
        scores = jnp.einsum('gqhd,gkhd->ghqk', query_blk.astype(jnp.float32), key_win.astype(jnp.float32)) * score_scale
        own_block = first_block + group_index * group_size + jnp.arange(group_size, dtype=jnp.int32)
        other_block = own_block[:, None] + other_shift[None, :]
        present = jnp.logical_and(other_block >= 0, other_block < block_total)
        allowed = jnp.logical_and(present[:, None, None, :], jnp.logical_not(excluded)[None, None, :, :])
        masked = jnp.where(allowed, scores, very_negative)
        row_max = lax.optimization_barrier(jnp.max(masked, axis=-1))
        weights = jnp.where(allowed, jnp.exp(masked - row_max[..., None]), 0.0)
        row_total = lax.optimization_barrier(jnp.sum(weights, axis=-1)) * 2.0 ** height
        weights_bf = lax.optimization_barrier(weights.astype(jnp.bfloat16))
        weighted = jnp.einsum('ghqk,gkhd->gqhd', weights_bf.astype(jnp.float32), value_win.astype(jnp.float32))
        return (jnp.transpose(row_max, (0, 2, 1)).reshape(group_size * block_rows, head_count), weighted.reshape(group_size * block_rows, col_count), jnp.transpose(row_total, (0, 2, 1)).reshape(group_size * block_rows, head_count))
    row_max, weighted, row_total = lax.map(one_group, jnp.arange(step_count, dtype=jnp.int32))
    return (row_max.reshape(row_count, head_count), weighted.reshape(row_count, col_count), row_total.reshape(row_count, head_count))

def merge_stats(finer, coarser):
    fine_max, fine_sum, fine_total = finer
    coarse_max, coarse_sum, coarse_total = coarser
    row_count, col_count = fine_sum.shape
    head_count = fine_max.shape[1]
    both_max = jnp.maximum(fine_max, coarse_max)
    fine_factor = jnp.exp(fine_max - both_max)
    coarse_factor = jnp.exp(coarse_max - both_max)
    merged = fine_sum.reshape(row_count, head_count, -1) * fine_factor[..., None] + coarse_sum.reshape(row_count, head_count, -1) * coarse_factor[..., None]
    return (both_max, merged.reshape(row_count, col_count), fine_total * fine_factor + coarse_total * coarse_factor)

def widen_stats(stats):
    return tuple((jnp.repeat(member, 2, axis=0) for member in stats))

def finish_output(stats):
    row_max, weighted, row_total = stats
    row_count, col_count = weighted.shape
    head_count = row_total.shape[1]
    return (weighted.reshape(row_count, head_count, -1) / row_total[..., None]).reshape(row_count, col_count).astype(jnp.bfloat16)

def reference(query_vecs, key_vecs, value_vecs):
    col_count = query_vecs.shape[1]
    query_rows, key_rows, value_rows = (query_vecs, key_vecs, value_vecs)
    all_stats = []
    for height in range(LEV):
        if height > 0:
            query_rows = coarsen_rows(query_rows, 0.5)
            key_rows = coarsen_rows(key_rows, 0.5)
            value_rows = coarsen_rows(value_rows, 1.0)
        block_count = query_rows.shape[0] // BLK
        border = jnp.zeros((BLK, col_count), key_rows.dtype)
        key_pad = jnp.concatenate([border, key_rows, border], axis=0)
        value_pad = jnp.concatenate([border, value_rows, border], axis=0)
        all_stats.append(attend_level(query_rows, key_pad, value_pad, height, HEAD_DIM, 0, block_count, BLK))
    running = all_stats[-1]
    for height in range(LEV - 2, -1, -1):
        running = merge_stats(all_stats[height], widen_stats(running))
    return finish_output(running)
```

```python
import math

import jax
import jax.numpy as jnp
from jax import lax
from jax.experimental import pallas as pl
from jax.experimental.pallas import tpu as pltpu
from jax.sharding import PartitionSpec as P

HEADS = 8
DIM = 128
BLK = 256
SLAB = 32
ROWS = 512
COLS = HEADS * DIM
NEG = -1e30
RATE = math.log2(math.e) / math.sqrt(DIM)
MESH = pl.DeviceIdType.MESH
BF = jnp.bfloat16
F32 = jnp.float32


def fold(value, factor):
    rows, width = value.shape
    paired = value.astype(F32).reshape(rows // (2 * SLAB), 2, SLAB, width)
    summed = paired[:, 0] + paired[:, 1]
    return (summed * factor).reshape(rows // 2, width).astype(BF)


def spread(value, times):
    rows, width = value.shape
    wide = jnp.broadcast_to(
        value.reshape(rows // SLAB, 1, SLAB, width), (rows // SLAB, times, SLAB, width)
    )
    return wide.reshape(rows * times, width)


def attend(query, keys, values, weight, bias=None):
    scores = lax.dot_general(
        query, keys, (((1,), (1,)), ((), ())), preferred_element_type=F32
    )
    if bias is not None:
        scores = scores + bias
    peak = jnp.max(scores, axis=1, keepdims=True)
    probs = jnp.exp2((scores - peak) * RATE).astype(BF)
    tail = jnp.full((values.shape[0], DIM), weight, BF)
    both = jnp.dot(probs, jnp.concatenate([values, tail], axis=1), preferred_element_type=F32)
    return jnp.broadcast_to(peak, (peak.shape[0], DIM)), both


def kernel(
    count,
    q_hbm,
    k_hbm,
    v_hbm,
    o_hbm,
    q0,
    kv0,
    qs,
    q1,
    q2,
    q3,
    kv1,
    kv3,
    perm,
    back,
    far0,
    far1,
    near0,
    near1,
    n2,
    x2,
    p2,
    px,
    x3,
    p3,
    acc,
    top,
    out,
    in_sem,
    halo0_send,
    halo0_recv,
    halo1_send,
    halo1_recv,
    n2_send,
    n2_recv,
    px_send,
    px_recv,
    x3_send,
    x3_recv,
    p3_send,
    p3_recv,
    out_sem,
):
    groups = count // 4
    seq = lax.axis_index("seq")
    grp = lax.axis_index("grp")
    me = seq * 4 + grp
    odd = grp % 2
    high = grp // 2

    def spot(index):
        wrapped = (index + count) % count
        return (wrapped // 4, wrapped % 4)

    far_dev = spot(me - 1 + 2 * odd)
    near_dev = spot(me + 1 - 2 * odd)
    skip_to = spot(me - 4 + 8 * odd)
    seq_prev = ((seq + groups - 1) % groups, grp)
    seq_next = ((seq + 1) % groups, grp)
    cross_dev = ((seq + groups + 1 - 2 * high) % groups, 3 - grp)

    loads = [
        pltpu.make_async_copy(k_hbm, kv0.at[0], in_sem.at[0]),
        pltpu.make_async_copy(v_hbm, kv0.at[1], in_sem.at[1]),
        pltpu.make_async_copy(q_hbm, q0, in_sem.at[2]),
    ]
    for load in loads:
        load.start()

    barrier = pltpu.get_barrier_semaphore()
    others = (far_dev, near_dev, seq_prev, seq_next, cross_dev)
    for other in others:
        pl.semaphore_signal(barrier, inc=1, device_id=other, device_id_type=MESH)

    row = lax.broadcasted_iota(jnp.int32, (BLK, BLK), 0)
    col = lax.broadcasted_iota(jnp.int32, (BLK, BLK), 1)
    perm[...] = jnp.where((row % SLAB) * 8 + row // SLAB == col, 1.0, 0.0).astype(BF)
    back[...] = jnp.where((col % SLAB) * 8 + col // SLAB == row, 1.0, 0.0).astype(BF)

    far_blk = odd
    near_blk = 1 - odd

    def columns(head):
        return pl.ds(pl.multiple_of(head * DIM, DIM), DIM)

    def halo0(side, kv, head):
        blk = (far_blk, near_blk)[side]
        return pltpu.make_async_remote_copy(
            src_ref=kv0.at[kv, pl.ds(pl.multiple_of(blk * BLK, BLK), BLK), columns(head)],
            dst_ref=(far0, near0)[side].at[head, kv],
            send_sem=halo0_send.at[side, kv, head],
            recv_sem=halo0_recv.at[side, kv, head],
            device_id=(far_dev, near_dev)[side],
            device_id_type=MESH,
        )

    def halo1(side, head):
        half = 1 - (far_blk, near_blk)[side]
        return pltpu.make_async_remote_copy(
            src_ref=kv1.at[head, half],
            dst_ref=(far1, near1)[side].at[head],
            send_sem=halo1_send.at[side, head],
            recv_sem=halo1_recv.at[side, head],
            device_id=(far_dev, near_dev)[side],
            device_id_type=MESH,
        )

    def n2_copy(leg, head):
        return pltpu.make_async_remote_copy(
            src_ref=n2.at[head],
            dst_ref=(p2, x2)[leg].at[head],
            send_sem=n2_send.at[leg, head],
            recv_sem=n2_recv.at[leg, head],
            device_id=(near_dev, skip_to)[leg],
            device_id_type=MESH,
        )

    def px_copy(head):
        return pltpu.make_async_remote_copy(
            src_ref=x2.at[head],
            dst_ref=px.at[head],
            send_sem=px_send.at[head],
            recv_sem=px_recv.at[head],
            device_id=near_dev,
            device_id_type=MESH,
        )

    def x3_copy(slot):
        return pltpu.make_async_remote_copy(
            src_ref=kv3,
            dst_ref=x3.at[slot],
            send_sem=x3_send.at[slot],
            recv_sem=x3_recv.at[slot],
            device_id=(seq_next, seq_prev, cross_dev)[slot],
            device_id_type=MESH,
        )

    def p3_copy(slot):
        return pltpu.make_async_remote_copy(
            src_ref=x3.at[slot],
            dst_ref=p3.at[slot],
            send_sem=p3_send.at[slot],
            recv_sem=p3_recv.at[slot],
            device_id=near_dev,
            device_id_type=MESH,
        )

    def out_copy(head):
        return pltpu.make_async_copy(out.at[head], o_hbm.at[:, columns(head)], out_sem.at[head])

    loads[0].wait()
    loads[1].wait()
    pl.semaphore_wait(barrier, len(others))

    for head in range(2):
        for kv in range(2):
            halo0(0, kv, head).start()
    for head in range(2):
        for kv in range(2):
            halo0(1, kv, head).start()

    def coarsen_head(head, carry):
        for kv in range(2):
            factor = (0.5, 1.0)[kv]
            for half in range(2):
                natural = kv0[kv, half * BLK : (half + 1) * BLK, columns(head)]
                slabs = jnp.dot(perm[...], natural, preferred_element_type=F32)
                first = fold(slabs, factor)
                kv1[head, half, kv] = first
                third = fold(fold(first, factor), factor)
                kv3[kv, head, half * SLAB : (half + 1) * SLAB, :] = third
        return carry

    lax.fori_loop(0, HEADS, coarsen_head, 0)

    for slot in range(3):
        x3_copy(slot).start()

    def send_head(head, carry):
        for side in range(2):
            halo1(side, head).start()

        @pl.when(head < HEADS - 2)
        def _():
            for side in range(2):
                for kv in range(2):
                    halo0(side, kv, head + 2).start()

        return carry

    lax.fori_loop(0, HEADS, send_head, 0)

    loads[2].wait()

    def query_head(head, carry):
        for half in range(2):
            natural = q0[half * BLK : (half + 1) * BLK, columns(head)]
            slabs = jnp.dot(perm[...], natural, preferred_element_type=F32)
            qs[head, half * BLK : (half + 1) * BLK, :] = slabs.astype(BF)
            first = fold(slabs, 0.5)
            second = fold(first, 0.5)
            third = fold(second, 0.5)
            q1[head, half] = first
            q2[head, half * 64 : (half + 1) * 64, :] = second
            q3[head, half * SLAB : (half + 1) * SLAB, :] = third
        return carry

    lax.fori_loop(0, HEADS, query_head, 0)

    def merge(head, start, rows, peak, both):
        where = pl.ds(pl.multiple_of(start, SLAB), rows)
        old = top[head, where, :]
        new = jnp.maximum(old, peak)
        old_scale = jnp.exp2((old - new) * RATE)
        new_scale = jnp.exp2((peak - new) * RATE)
        acc[head, where, :DIM] = acc[head, where, :DIM] * old_scale + both[:, :DIM] * new_scale
        acc[head, where, DIM:] = acc[head, where, DIM:] * old_scale + both[:, DIM:] * new_scale
        top[head, where, :] = new

    def side_terms(head, blk, fine, coarse, bias):
        keys, values = fine[head, 0], fine[head, 1]
        sums_k = fold(jnp.dot(perm[...], keys, preferred_element_type=F32), 0.5)
        sums_v = fold(jnp.dot(perm[...], values, preferred_element_type=F32), 1.0)
        start = blk * BLK
        query = qs[head, pl.ds(pl.multiple_of(start, BLK), BLK), :]
        peak, both = attend(query, keys, values, 1.0)
        merge(head, start, BLK, peak + bias, both)
        rest_k, rest_v = coarse[head, 0], coarse[head, 1]
        peak, both = attend(q1[head, blk], rest_k, rest_v, 2.0)
        merge(head, start, BLK, spread(peak + bias, 2), spread(both, 2))
        peak, both = attend(
            q1[head, 1 - blk],
            jnp.concatenate([rest_k, sums_k], axis=0),
            jnp.concatenate([rest_v, sums_v], axis=0),
            2.0,
        )
        merge(head, (1 - blk) * BLK, BLK, spread(peak + bias, 2), spread(both, 2))
        return sums_k, sums_v

    def own_head(head, carry):
        keys = kv0[0, :, columns(head)]
        values = kv0[1, :, columns(head)]
        for part in range(4):
            where = slice(part * 128, (part + 1) * 128)
            peak, both = attend(qs[head, where, :], keys, values, 1.0)
            acc[head, where, :] = both
            top[head, where, :] = peak
        halo0(1, 0, head).wait_recv()
        halo0(1, 1, head).wait_recv()
        halo1(1, head).wait_recv()
        side_terms(head, near_blk, near0, near1, 0.0)
        return carry

    lax.fori_loop(0, HEADS, own_head, 0)

    for slot in range(3):
        x3_copy(slot).wait_recv()
        p3_copy(slot).start()
    for slot in range(3):
        p3_copy(slot).wait_recv()

    has_prev = jnp.where(seq > 0, 0.0, NEG)
    has_next = jnp.where(seq < groups - 1, 0.0, NEG)
    has_cross = jnp.where(high == 0, has_next, has_prev)

    def third_head(head, carry):
        keys = jnp.concatenate(
            [ref[slot, 0, head] for slot in range(3) for ref in (x3, p3)], axis=0
        )
        values = jnp.concatenate(
            [ref[slot, 1, head] for slot in range(3) for ref in (x3, p3)], axis=0
        )
        place = lax.broadcasted_iota(jnp.int32, (1, 3 * DIM), 1) // DIM
        bias = jnp.where(place == 0, has_prev, jnp.where(place == 1, has_next, has_cross))
        peak, both = attend(q3[head], keys, values, 8.0, bias)
        merge(head, 0, ROWS, spread(peak, 8), spread(both, 8))
        return carry

    lax.fori_loop(0, HEADS, third_head, 0)

    toward = 1 - 2 * odd

    def present(index):
        inside = jnp.logical_and(index >= 0, index < count)
        return jnp.where(inside, 0.0, NEG)

    far_bias = present(me - toward)
    x2_bias = present(me + 3 * toward)
    p2_bias = present(me + 2 * toward)
    px_bias = present(me - 2 * toward)

    def finish(head):
        px_copy(head).wait_recv()
        n2_copy(0, head).wait_recv()
        keys = jnp.concatenate([x2[head, 0], p2[head, 0], px[head, 0]], axis=0)
        values = jnp.concatenate([x2[head, 1], p2[head, 1], px[head, 1]], axis=0)
        place = lax.broadcasted_iota(jnp.int32, (1, 3 * DIM), 1) // DIM
        bias = jnp.where(place == 0, x2_bias, jnp.where(place == 1, p2_bias, px_bias))
        peak, both = attend(q2[head], keys, values, 4.0, bias)
        merge(head, 0, ROWS, spread(peak, 4), spread(both, 4))
        for half in range(2):
            where = slice(half * BLK, (half + 1) * BLK)
            ratio = (acc[head, where, :DIM] / acc[head, where, DIM:]).astype(BF)
            out[head, where, :] = jnp.dot(
                back[...], ratio, preferred_element_type=F32
            ).astype(BF)
        out_copy(head).start()

    def relay(head):
        n2_copy(1, head).wait_recv()
        px_copy(head).start()

    def far_head(head, carry):
        halo0(0, 0, head).wait_recv()
        halo0(0, 1, head).wait_recv()
        halo1(0, head).wait_recv()
        for kv in range(2):
            factor = (0.5, 1.0)[kv]
            slabs = jnp.dot(perm[...], far0[head, kv], preferred_element_type=F32)
            n2[head, kv, 0:64, :] = fold(fold(slabs, factor), factor)
            n2[head, kv, 64:128, :] = fold(far1[head, kv], factor)
        n2_copy(0, head).start()
        n2_copy(1, head).start()

        @pl.when(head > 0)
        def _():
            relay(head - 1)

        side_terms(head, far_blk, far0, far1, far_bias)

        @pl.when(head > 0)
        def _():
            finish(head - 1)

        return carry

    lax.fori_loop(0, HEADS, far_head, 0)
    relay(HEADS - 1)
    finish(HEADS - 1)

    def drain(head, carry):
        for side in range(2):
            for kv in range(2):
                halo0(side, kv, head).wait_send()
            halo1(side, head).wait_send()
        n2_copy(0, head).wait_send()
        n2_copy(1, head).wait_send()
        px_copy(head).wait_send()
        out_copy(head).wait()
        return carry

    lax.fori_loop(0, HEADS, drain, 0)
    for slot in range(3):
        x3_copy(slot).wait_send()
        p3_copy(slot).wait_send()


def solution(mesh):
    count = mesh.shape["seq"] * mesh.shape["grp"]

    def local(query_vecs, key_vecs, value_vecs):
        anywhere = pl.BlockSpec(memory_space=pl.ANY)
        dma = pltpu.SemaphoreType.DMA
        return pl.pallas_call(
            lambda *refs: kernel(count, *refs),
            out_shape=jax.ShapeDtypeStruct((ROWS, COLS), BF),
            in_specs=[anywhere] * 3,
            out_specs=anywhere,
            scratch_shapes=[
                pltpu.VMEM((ROWS, COLS), BF),
                pltpu.VMEM((2, ROWS, COLS), BF),
                pltpu.VMEM((HEADS, ROWS, DIM), BF),
                pltpu.VMEM((HEADS, 2, 128, DIM), BF),
                pltpu.VMEM((HEADS, 128, DIM), BF),
                pltpu.VMEM((HEADS, 64, DIM), BF),
                pltpu.VMEM((HEADS, 2, 2, 128, DIM), BF),
                pltpu.VMEM((2, HEADS, 64, DIM), BF),
                pltpu.VMEM((BLK, BLK), BF),
                pltpu.VMEM((BLK, BLK), BF),
                pltpu.VMEM((HEADS, 2, BLK, DIM), BF),
                pltpu.VMEM((HEADS, 2, 128, DIM), BF),
                pltpu.VMEM((HEADS, 2, BLK, DIM), BF),
                pltpu.VMEM((HEADS, 2, 128, DIM), BF),
                pltpu.VMEM((HEADS, 2, 128, DIM), BF),
                pltpu.VMEM((HEADS, 2, 128, DIM), BF),
                pltpu.VMEM((HEADS, 2, 128, DIM), BF),
                pltpu.VMEM((HEADS, 2, 128, DIM), BF),
                pltpu.VMEM((3, 2, HEADS, 64, DIM), BF),
                pltpu.VMEM((3, 2, HEADS, 64, DIM), BF),
                pltpu.VMEM((HEADS, ROWS, 2 * DIM), F32),
                pltpu.VMEM((HEADS, ROWS, DIM), F32),
                pltpu.VMEM((HEADS, ROWS, DIM), BF),
                dma((3,)),
                dma((2, 2, HEADS)),
                dma((2, 2, HEADS)),
                dma((2, HEADS)),
                dma((2, HEADS)),
                dma((2, HEADS)),
                dma((2, HEADS)),
                dma((HEADS,)),
                dma((HEADS,)),
                dma((3,)),
                dma((3,)),
                dma((3,)),
                dma((3,)),
                dma((HEADS,)),
            ],
            compiler_params=pltpu.CompilerParams(
                collective_id=0, has_side_effects=True, vmem_limit_bytes=48 * 1024 * 1024
            ),
        )(query_vecs, key_vecs, value_vecs)

    spec = P(("seq", "grp"), None)
    return jax.shard_map(
        local, mesh=mesh, in_specs=(spec, spec, spec), out_specs=spec, check_vma=False
    )
```

```python
import math

import jax
import jax.numpy as jnp
from jax import lax
from jax.experimental import pallas as pl
from jax.experimental.pallas import tpu as pltpu
from jax.sharding import PartitionSpec as P

HEADS = 8
DIM = 128
BLK = 256
SLAB = 32
ROWS = 512
COLS = HEADS * DIM
NEG = -1e30
RELAY_LAG = 2
FINISH_LAG = 3
WINDOW = 3
RATE = math.log2(math.e) / math.sqrt(DIM)
MESH = pl.DeviceIdType.MESH
BF = jnp.bfloat16
F32 = jnp.float32


def fold(value, factor):
    rows, width = value.shape
    paired = value.astype(F32).reshape(rows // (2 * SLAB), 2, SLAB, width)
    summed = paired[:, 0] + paired[:, 1]
    return (summed * factor).reshape(rows // 2, width).astype(BF)


def spread(value, times):
    rows, width = value.shape
    wide = jnp.broadcast_to(
        value.reshape(rows // SLAB, 1, SLAB, width), (rows // SLAB, times, SLAB, width)
    )
    return wide.reshape(rows * times, width)


def attend(query, parts, weight):
    scores = []
    peak = None
    for keys, _, bias in parts:
        block = lax.dot_general(
            query, keys, (((1,), (1,)), ((), ())), preferred_element_type=F32
        )
        if bias is not None:
            block = block + bias
        scores.append(block)
        for start in range(0, block.shape[1], DIM):
            piece = block[:, start : start + DIM]
            peak = piece if peak is None else jnp.maximum(peak, piece)
    peak = jnp.max(peak, axis=1, keepdims=True)
    both = None
    for block, (_, values, _) in zip(scores, parts):
        probs = jnp.exp2((block - peak) * RATE).astype(BF)
        tail = jnp.full((values.shape[0], DIM), weight, BF)
        term = jnp.dot(
            probs, jnp.concatenate([values, tail], axis=1), preferred_element_type=F32
        )
        both = term if both is None else both + term
    return jnp.broadcast_to(peak, (peak.shape[0], DIM)), both


def when(condition, action):
    if condition is None:
        action()
    else:
        pl.when(condition)(action)


def kernel(
    count,
    q_hbm,
    k_hbm,
    v_hbm,
    o_hbm,
    q0,
    kv0,
    qs,
    q1,
    q2,
    q3,
    kv1,
    kv3,
    perm,
    back,
    far0,
    far1,
    near0,
    near1,
    kv2,
    n2,
    x2,
    p2,
    px,
    x3,
    p3,
    acc,
    top,
    acc1,
    top1,
    out,
    in_sem,
    halo0_send,
    halo0_recv,
    halo1_send,
    halo1_recv,
    n2_send,
    n2_recv,
    px_send,
    px_recv,
    x3_send,
    x3_recv,
    p3_send,
    p3_recv,
    out_sem,
    own_send,
    turn_send,
):
    groups = count // 4
    seq = lax.axis_index("seq")
    grp = lax.axis_index("grp")
    me = seq * 4 + grp
    odd = grp % 2
    high = grp // 2

    def spot(index):
        wrapped = (index + count) % count
        return (wrapped // 4, wrapped % 4)

    far_dev = spot(me - 1 + 2 * odd)
    near_dev = spot(me + 1 - 2 * odd)
    skip_to = spot(me - 4 + 8 * odd)
    direct_dev = spot(me + 3 - 6 * odd)
    mirror_dev = (seq, 3 - grp)
    seq_prev = ((seq + groups - 1) % groups, grp)
    seq_next = ((seq + 1) % groups, grp)
    cross_dev = ((seq + groups + 1 - 2 * high) % groups, 3 - grp)

    loads = [
        pltpu.make_async_copy(k_hbm, kv0.at[0], in_sem.at[0]),
        pltpu.make_async_copy(v_hbm, kv0.at[1], in_sem.at[1]),
        pltpu.make_async_copy(q_hbm, q0, in_sem.at[2]),
    ]
    for load in loads:
        load.start()

    last = groups - 1
    edge = jnp.logical_or(seq == 0, seq == last)
    has_far = jnp.logical_and(me > 0, me < count - 1)
    has_prev = seq > 0
    has_next = seq < last
    has_cross = jnp.where(high == 0, seq < last, seq > 0)
    wrap_next = jnp.logical_and(seq % 4 == 3, has_next)
    wrap_prev = jnp.logical_and(seq % 4 == 0, has_prev)
    wraps = jnp.logical_or(wrap_next, wrap_prev)
    turned = jnp.logical_or(
        jnp.logical_and(grp == 2, wrap_next), jnp.logical_and(grp == 1, wrap_prev)
    )
    gives_own = jnp.logical_or(turned, jnp.logical_or(me == 0, me == count - 1))
    meets_own = jnp.logical_or(gives_own, jnp.logical_or(me == 3, me == count - 4))
    inner = jnp.where(odd == 0, seq > 0, seq < last)
    gives_skip = jnp.logical_and(
        inner,
        jnp.logical_not(
            jnp.logical_or(
                jnp.logical_and(grp == 2, wrap_prev), jnp.logical_and(grp == 1, wrap_next)
            )
        ),
    )
    takes_skip = jnp.logical_or(
        jnp.where(odd == 0, seq < last, seq > 0), jnp.logical_or(me == 3, me == count - 4)
    )
    mate_skip = jnp.logical_or(inner, jnp.logical_or(me == 2, me == count - 3))
    gives_turn = jnp.where(high == 0, wrap_next, wrap_prev)
    mate_far = jnp.where(odd == 0, me + 1 < count - 1, me > 1)

    @pl.when(edge)
    def _():
        for ref in (far0, far1, x2, p2, px, x3, p3):
            ref[...] = jnp.zeros_like(ref)

    barrier = pltpu.get_barrier_semaphore()
    links = (
        (far_dev, has_far),
        (near_dev, None),
        (seq_prev, has_prev),
        (seq_next, has_next),
        (cross_dev, has_cross),
        (direct_dev, meets_own),
        (mirror_dev, jnp.logical_and(wraps, odd == high)),
    )
    for other, exists in links:
        when(exists, lambda: pl.semaphore_signal(
            barrier, inc=1, device_id=other, device_id_type=MESH
        ))

    row = lax.broadcasted_iota(jnp.int32, (BLK, BLK), 0)
    col = lax.broadcasted_iota(jnp.int32, (BLK, BLK), 1)
    perm[...] = jnp.where((row % SLAB) * 8 + row // SLAB == col, 1.0, 0.0).astype(BF)
    back[...] = jnp.where((col % SLAB) * 8 + col // SLAB == row, 1.0, 0.0).astype(BF)

    far_blk = odd
    near_blk = 1 - odd

    def columns(head):
        return pl.ds(pl.multiple_of(head * DIM, DIM), DIM)

    def halo0(side, kv, head):
        blk = (far_blk, near_blk)[side]
        return pltpu.make_async_remote_copy(
            src_ref=kv0.at[kv, pl.ds(pl.multiple_of(blk * BLK, BLK), BLK), columns(head)],
            dst_ref=(far0, near0)[side].at[head, kv],
            send_sem=halo0_send.at[side, kv, head],
            recv_sem=halo0_recv.at[side, kv, head],
            device_id=(far_dev, near_dev)[side],
            device_id_type=MESH,
        )

    def halo1(side, head):
        half = 1 - (far_blk, near_blk)[side]
        return pltpu.make_async_remote_copy(
            src_ref=kv1.at[head, half],
            dst_ref=(far1, near1)[side].at[head],
            send_sem=halo1_send.at[side, head],
            recv_sem=halo1_recv.at[side, head],
            device_id=(far_dev, near_dev)[side],
            device_id_type=MESH,
        )

    def n2_copy(leg, head):
        return pltpu.make_async_remote_copy(
            src_ref=n2.at[head],
            dst_ref=(p2, x2)[leg].at[head],
            send_sem=n2_send.at[leg, head],
            recv_sem=n2_recv.at[leg, head],
            device_id=(near_dev, skip_to)[leg],
            device_id_type=MESH,
        )

    def px_copy(head):
        return pltpu.make_async_remote_copy(
            src_ref=x2.at[head],
            dst_ref=px.at[head],
            send_sem=px_send.at[head],
            recv_sem=px_recv.at[head],
            device_id=near_dev,
            device_id_type=MESH,
        )

    def x3_copy(slot):
        return pltpu.make_async_remote_copy(
            src_ref=kv3,
            dst_ref=x3.at[slot],
            send_sem=x3_send.at[slot],
            recv_sem=x3_recv.at[slot],
            device_id=(seq_next, seq_prev, cross_dev)[slot],
            device_id_type=MESH,
        )

    def turn_copy():
        return pltpu.make_async_remote_copy(
            src_ref=x3.at[2],
            dst_ref=x3.at[1 - high],
            send_sem=turn_send,
            recv_sem=x3_recv.at[1 - high],
            device_id=mirror_dev,
            device_id_type=MESH,
        )

    def own_copy(head):
        return pltpu.make_async_remote_copy(
            src_ref=kv2.at[head],
            dst_ref=x2.at[head],
            send_sem=own_send.at[head],
            recv_sem=n2_recv.at[1, head],
            device_id=direct_dev,
            device_id_type=MESH,
        )

    def p3_copy(slot):
        return pltpu.make_async_remote_copy(
            src_ref=x3.at[slot],
            dst_ref=p3.at[slot],
            send_sem=p3_send.at[slot],
            recv_sem=p3_recv.at[slot],
            device_id=near_dev,
            device_id_type=MESH,
        )

    def out_copy(head):
        return pltpu.make_async_copy(out.at[head], o_hbm.at[:, columns(head)], out_sem.at[head])

    loads[0].wait()
    loads[1].wait()
    peers = sum(1 if exists is None else jnp.where(exists, 1, 0) for _, exists in links)
    pl.semaphore_wait(barrier, peers)

    @pl.when(has_far)
    def _():
        for head in range(2):
            for kv in range(2):
                halo0(0, kv, head).start()

    for head in range(2):
        for kv in range(2):
            halo0(1, kv, head).start()

    def pair_columns(pair):
        return pl.ds(pl.multiple_of(pair * 2 * DIM, 2 * DIM), 2 * DIM)

    def coarsen_pair(pair, carry):
        for kv in range(2):
            factor = (0.5, 1.0)[kv]
            for half in range(2):
                natural = kv0[kv, half * BLK : (half + 1) * BLK, pair_columns(pair)]
                slabs = jnp.dot(perm[...], natural, preferred_element_type=F32)
                first = fold(slabs, factor)
                second = fold(first, factor)
                third = fold(second, factor)
                for sub in range(2):
                    head = 2 * pair + sub
                    lanes = slice(sub * DIM, (sub + 1) * DIM)
                    kv1[head, half, kv] = first[:, lanes]
                    kv2[head, kv, half * 64 : (half + 1) * 64, :] = second[:, lanes]
                    kv3[kv, head, half * SLAB : (half + 1) * SLAB, :] = third[:, lanes]
        return carry

    lax.fori_loop(0, HEADS // 2, coarsen_pair, 0)

    third_to = (
        jnp.logical_and(has_next, jnp.logical_not(jnp.logical_and(wrap_next, high == 0))),
        jnp.logical_and(has_prev, jnp.logical_not(jnp.logical_and(wrap_prev, high == 1))),
        has_cross,
    )
    third_from = (has_prev, has_next, has_cross)
    for slot in range(3):
        when(third_to[slot], lambda: x3_copy(slot).start())

    def send_side(side, head):
        for kv in range(2):
            halo0(side, kv, head).start()
        halo1(side, head).start()

    @pl.when(has_far)
    def _():
        halo1(0, 0).start()
        halo1(0, 1).start()
        for head in range(2, WINDOW):
            send_side(0, head)

    @pl.when(gives_own)
    def _():
        lax.fori_loop(0, HEADS, lambda head, c: (own_copy(head).start(), c)[1], 0)

    halo1(1, 0).start()
    halo1(1, 1).start()
    lax.fori_loop(2, HEADS, lambda head, c: (send_side(1, head), c)[1], 0)

    loads[2].wait()

    def query_pair(pair, carry):
        for half in range(2):
            natural = q0[half * BLK : (half + 1) * BLK, pair_columns(pair)]
            slabs = jnp.dot(perm[...], natural, preferred_element_type=F32)
            first = fold(slabs, 0.5)
            second = fold(first, 0.5)
            third = fold(second, 0.5)
            for sub in range(2):
                head = 2 * pair + sub
                lanes = slice(sub * DIM, (sub + 1) * DIM)
                qs[head, half * BLK : (half + 1) * BLK, :] = slabs[:, lanes].astype(BF)
                q1[head, half] = first[:, lanes]
                q2[head, half * 64 : (half + 1) * 64, :] = second[:, lanes]
                q3[head, half * SLAB : (half + 1) * SLAB, :] = third[:, lanes]
        return carry

    lax.fori_loop(0, HEADS // 2, query_pair, 0)

    def hidden(exists):
        return jnp.where(exists, 0.0, NEG)

    far_bias = hidden(has_far)
    x2_bias = hidden(takes_skip)
    p2_bias = hidden(mate_far)
    px_bias = hidden(mate_skip)
    third_bias = [hidden(exists) for exists in third_from]

    def half_rows(blk):
        return pl.ds(pl.multiple_of(blk * BLK, BLK), BLK)

    def fine_levels(head):
        sums = []
        for ref in (far0, near0):
            for kv in range(2):
                slabs = jnp.dot(perm[...], ref[head, kv], preferred_element_type=F32)
                sums.append(fold(slabs, (0.5, 1.0)[kv]))
        own = (kv0[0, :, columns(head)], kv0[1, :, columns(head)], None)
        far = (far0[head, 0], far0[head, 1], far_bias)
        near = (near0[head, 0], near0[head, 1], None)
        for blk, part in ((far_blk, far), (near_blk, near)):
            peak, both = attend(qs[head, half_rows(blk), :], (own, part), 1.0)
            acc[head, half_rows(blk), :] = both
            top[head, half_rows(blk), :] = peak
        far_rest = (far1[head, 0], far1[head, 1], far_bias)
        near_rest = (near1[head, 0], near1[head, 1], None)
        far_sums = (sums[0], sums[1], far_bias)
        near_sums = (sums[2], sums[3], None)
        for blk, part in ((far_blk, near_sums), (near_blk, far_sums)):
            peak, both = attend(q1[head, blk], (far_rest, near_rest, part), 2.0)
            acc1[head, blk] = both
            top1[head, blk] = peak

    def finish(head):
        keys = [ref[slot, 0, head] for slot in range(3) for ref in (x3, p3)]
        values = [ref[slot, 1, head] for slot in range(3) for ref in (x3, p3)]
        peak3, both3 = attend(
            q3[head],
            [
                (
                    jnp.concatenate(keys[2 * slot : 2 * slot + 2], axis=0),
                    jnp.concatenate(values[2 * slot : 2 * slot + 2], axis=0),
                    third_bias[slot],
                )
                for slot in range(3)
            ],
            8.0,
        )
        when(mate_skip, lambda: px_copy(head).wait_recv())
        when(mate_far, lambda: n2_copy(0, head).wait_recv())
        peak2, both2 = attend(
            q2[head],
            [
                (ref[head, 0], ref[head, 1], bias)
                for ref, bias in ((x2, x2_bias), (p2, p2_bias), (px, px_bias))
            ],
            4.0,
        )

        def join(peak_a, both_a, peak_b, both_b):
            peak = jnp.maximum(peak_a, peak_b)
            scale_a = jnp.exp2((peak_a - peak) * RATE)
            scale_b = jnp.exp2((peak_b - peak) * RATE)
            both = jnp.concatenate(
                [
                    both_a[:, :DIM] * scale_a + both_b[:, :DIM] * scale_b,
                    both_a[:, DIM:] * scale_a + both_b[:, DIM:] * scale_b,
                ],
                axis=1,
            )
            return peak, both

        peak2, both2 = join(peak2, both2, spread(peak3, 2), spread(both3, 2))
        for half in range(2):
            rows2 = slice(half * 64, (half + 1) * 64)
            peak1, both1 = join(
                top1[head, half],
                acc1[head, half],
                spread(peak2[rows2], 2),
                spread(both2[rows2], 2),
            )
            rows = slice(half * BLK, (half + 1) * BLK)
            _, both = join(
                top[head, rows, :], acc[head, rows, :], spread(peak1, 2), spread(both1, 2)
            )
            ratio = (both[:, :DIM] / both[:, DIM:]).astype(BF)
            out[head, rows, :] = jnp.dot(
                back[...], ratio, preferred_element_type=F32
            ).astype(BF)
        out_copy(head).start()

    def send_second(head):
        for kv in range(2):
            factor = (0.5, 1.0)[kv]
            slabs = jnp.dot(perm[...], far0[head, kv], preferred_element_type=F32)
            n2[head, kv, 0:64, :] = fold(fold(slabs, factor), factor)
            n2[head, kv, 64:128, :] = fold(far1[head, kv], factor)
        n2_copy(0, head).start()
        when(gives_skip, lambda: n2_copy(1, head).start())

    def relay(head):
        n2_copy(1, head).wait_recv()
        px_copy(head).start()

    def each_head(head, carry):
        @pl.when(has_far)
        def _():
            halo0(0, 0, head).wait_recv()
            halo0(0, 1, head).wait_recv()
            halo1(0, head).wait_recv()
            when(head < HEADS - WINDOW, lambda: send_side(0, head + WINDOW))
            send_second(head)

        when(
            jnp.logical_and(takes_skip, head >= RELAY_LAG), lambda: relay(head - RELAY_LAG)
        )
        halo0(1, 0, head).wait_recv()
        halo0(1, 1, head).wait_recv()
        halo1(1, head).wait_recv()
        fine_levels(head)

        @pl.when(head == FINISH_LAG - 1)
        def _():
            for slot in (2, 0, 1):

                @pl.when(third_from[slot])
                def _():
                    x3_copy(slot).wait_recv()
                    if slot == 2:
                        when(gives_turn, lambda: turn_copy().start())
                    p3_copy(slot).start()

        @pl.when(head == FINISH_LAG)
        def _():
            for slot in range(3):
                when(third_from[slot], lambda: p3_copy(slot).wait_recv())

        @pl.when(head >= FINISH_LAG)
        def _():
            finish(head - FINISH_LAG)

        return carry

    lax.fori_loop(0, HEADS, each_head, 0)

    def trail(head, carry):
        when(
            jnp.logical_and(takes_skip, head + FINISH_LAG - RELAY_LAG < HEADS),
            lambda: relay(head + FINISH_LAG - RELAY_LAG),
        )
        finish(head)
        return carry

    lax.fori_loop(HEADS - FINISH_LAG, HEADS, trail, 0)

    def drain(head, carry):
        @pl.when(has_far)
        def _():
            for kv in range(2):
                halo0(0, kv, head).wait_send()
            halo1(0, head).wait_send()
            n2_copy(0, head).wait_send()

        for kv in range(2):
            halo0(1, kv, head).wait_send()
        halo1(1, head).wait_send()
        when(gives_skip, lambda: n2_copy(1, head).wait_send())
        when(gives_own, lambda: own_copy(head).wait_send())
        when(takes_skip, lambda: px_copy(head).wait_send())
        out_copy(head).wait()
        return carry

    lax.fori_loop(0, HEADS, drain, 0)
    for slot in range(3):
        when(third_to[slot], lambda: x3_copy(slot).wait_send())
        when(third_from[slot], lambda: p3_copy(slot).wait_send())
    when(gives_turn, lambda: turn_copy().wait_send())


def solution(mesh):
    count = mesh.shape["seq"] * mesh.shape["grp"]

    def local(query_vecs, key_vecs, value_vecs):
        anywhere = pl.BlockSpec(memory_space=pl.ANY)
        dma = pltpu.SemaphoreType.DMA
        return pl.pallas_call(
            lambda *refs: kernel(count, *refs),
            out_shape=jax.ShapeDtypeStruct((ROWS, COLS), BF),
            in_specs=[anywhere] * 3,
            out_specs=anywhere,
            scratch_shapes=[
                pltpu.VMEM((ROWS, COLS), BF),
                pltpu.VMEM((2, ROWS, COLS), BF),
                pltpu.VMEM((HEADS, ROWS, DIM), BF),
                pltpu.VMEM((HEADS, 2, 128, DIM), BF),
                pltpu.VMEM((HEADS, 128, DIM), BF),
                pltpu.VMEM((HEADS, 64, DIM), BF),
                pltpu.VMEM((HEADS, 2, 2, 128, DIM), BF),
                pltpu.VMEM((2, HEADS, 64, DIM), BF),
                pltpu.VMEM((BLK, BLK), BF),
                pltpu.VMEM((BLK, BLK), BF),
                pltpu.VMEM((HEADS, 2, BLK, DIM), BF),
                pltpu.VMEM((HEADS, 2, 128, DIM), BF),
                pltpu.VMEM((HEADS, 2, BLK, DIM), BF),
                pltpu.VMEM((HEADS, 2, 128, DIM), BF),
                pltpu.VMEM((HEADS, 2, 128, DIM), BF),
                pltpu.VMEM((HEADS, 2, 128, DIM), BF),
                pltpu.VMEM((HEADS, 2, 128, DIM), BF),
                pltpu.VMEM((HEADS, 2, 128, DIM), BF),
                pltpu.VMEM((HEADS, 2, 128, DIM), BF),
                pltpu.VMEM((3, 2, HEADS, 64, DIM), BF),
                pltpu.VMEM((3, 2, HEADS, 64, DIM), BF),
                pltpu.VMEM((HEADS, ROWS, 2 * DIM), F32),
                pltpu.VMEM((HEADS, ROWS, DIM), F32),
                pltpu.VMEM((HEADS, 2, 128, 2 * DIM), F32),
                pltpu.VMEM((HEADS, 2, 128, DIM), F32),
                pltpu.VMEM((HEADS, ROWS, DIM), BF),
                dma((3,)),
                dma((2, 2, HEADS)),
                dma((2, 2, HEADS)),
                dma((2, HEADS)),
                dma((2, HEADS)),
                dma((2, HEADS)),
                dma((2, HEADS)),
                dma((HEADS,)),
                dma((HEADS,)),
                dma((3,)),
                dma((3,)),
                dma((3,)),
                dma((3,)),
                dma((HEADS,)),
                dma((HEADS,)),
                dma,
            ],
            compiler_params=pltpu.CompilerParams(
                collective_id=0, has_side_effects=True, vmem_limit_bytes=63 * 1024 * 1024
            ),
        )(query_vecs, key_vecs, value_vecs)

    spec = P(("seq", "grp"), None)
    return jax.shard_map(
        local, mesh=mesh, in_specs=(spec, spec, spec), out_specs=spec, check_vma=False
    )
```

```python
import math

import jax
import jax.numpy as jnp
from jax import lax
from jax.experimental import pallas as pl
from jax.experimental.pallas import tpu as pltpu
from jax.sharding import PartitionSpec as P

HEADS = 8
DIM = 128
BLK = 256
SLAB = 32
ROWS = 512
COLS = HEADS * DIM
NEG = -1e30
RELAY_LAG = 2
TURN_LAG = 1
STREAM_LAG = 3
FINISH_LAG = 4
DIAGONAL_WINDOW = 3
STRAIGHT_WINDOW = 5
RATE = math.log2(math.e) / math.sqrt(DIM)
MESH = pl.DeviceIdType.MESH
BF = jnp.bfloat16
F32 = jnp.float32


def fold(value, factor):
    rows, width = value.shape
    paired = value.astype(F32).reshape(rows // (2 * SLAB), 2, SLAB, width)
    summed = paired[:, 0] + paired[:, 1]
    return (summed * factor).reshape(rows // 2, width).astype(BF)


def spread(value, times):
    rows, width = value.shape
    wide = jnp.broadcast_to(
        value.reshape(rows // SLAB, 1, SLAB, width), (rows // SLAB, times, SLAB, width)
    )
    return wide.reshape(rows * times, width)


def attend(query, parts, weight):
    scores = []
    peak = None
    for keys, _, bias in parts:
        block = lax.dot_general(
            query, keys, (((1,), (1,)), ((), ())), preferred_element_type=F32
        )
        if bias is not None:
            block = block + bias
        scores.append(block)
        for start in range(0, block.shape[1], DIM):
            piece = block[:, start : start + DIM]
            peak = piece if peak is None else jnp.maximum(peak, piece)
    peak = jnp.max(peak, axis=1, keepdims=True)
    both = None
    for block, (_, values, _) in zip(scores, parts):
        probs = jnp.exp2((block - peak) * RATE).astype(BF)
        tail = jnp.full((values.shape[0], DIM), weight, BF)
        term = jnp.dot(
            probs, jnp.concatenate([values, tail], axis=1), preferred_element_type=F32
        )
        both = term if both is None else both + term
    return jnp.broadcast_to(peak, (peak.shape[0], DIM)), both


def when(condition, action):
    if condition is None:
        action()
    else:
        pl.when(condition)(action)


def kernel(
    count,
    q_hbm,
    k_hbm,
    v_hbm,
    o_hbm,
    q0,
    kv0,
    qs,
    q1,
    q2,
    q3,
    kv1,
    kv3,
    perm,
    back,
    far0,
    far1,
    near0,
    near1,
    kv2,
    n2,
    x2,
    p2,
    px,
    c3,
    x3,
    p3,
    acc,
    top,
    acc1,
    top1,
    out,
    in_sem,
    halo0_send,
    halo0_recv,
    halo1_send,
    halo1_recv,
    n2_send,
    n2_recv,
    px_send,
    px_recv,
    x3_send,
    x3_recv,
    p3_send,
    p3_recv,
    out_sem,
    own_send,
    turn_send,
    c3_send,
):
    groups = count // 4
    seq = lax.axis_index("seq")
    grp = lax.axis_index("grp")
    me = seq * 4 + grp
    odd = grp % 2
    high = grp // 2

    def spot(index):
        wrapped = (index + count) % count
        return (wrapped // 4, wrapped % 4)

    far_dev = spot(me - 1 + 2 * odd)
    near_dev = spot(me + 1 - 2 * odd)
    skip_to = spot(me - 4 + 8 * odd)
    direct_dev = spot(me + 3 - 6 * odd)
    mirror_dev = (seq, 3 - grp)
    seq_prev = ((seq + groups - 1) % groups, grp)
    seq_next = ((seq + 1) % groups, grp)
    cross_dev = ((seq + groups + 1 - 2 * high) % groups, 3 - grp)

    loads = [
        pltpu.make_async_copy(k_hbm, kv0.at[0], in_sem.at[0]),
        pltpu.make_async_copy(v_hbm, kv0.at[1], in_sem.at[1]),
        pltpu.make_async_copy(q_hbm, q0, in_sem.at[2]),
    ]
    for load in loads:
        load.start()

    last = groups - 1
    edge = jnp.logical_or(seq == 0, seq == last)
    has_far = jnp.logical_and(me > 0, me < count - 1)
    window = jnp.where(odd == high, DIAGONAL_WINDOW, STRAIGHT_WINDOW)
    has_prev = seq > 0
    has_next = seq < last
    has_cross = jnp.where(high == 0, seq < last, seq > 0)
    wrap_next = jnp.logical_and(seq % 4 == 3, has_next)
    wrap_prev = jnp.logical_and(seq % 4 == 0, has_prev)
    wraps = jnp.logical_or(wrap_next, wrap_prev)
    turned = jnp.logical_or(
        jnp.logical_and(grp == 2, wrap_next), jnp.logical_and(grp == 1, wrap_prev)
    )
    gives_own = jnp.logical_or(turned, jnp.logical_or(me == 0, me == count - 1))
    meets_own = jnp.logical_or(gives_own, jnp.logical_or(me == 3, me == count - 4))
    inner = jnp.where(odd == 0, seq > 0, seq < last)
    gives_skip = jnp.logical_and(
        inner,
        jnp.logical_not(
            jnp.logical_or(
                jnp.logical_and(grp == 2, wrap_prev), jnp.logical_and(grp == 1, wrap_next)
            )
        ),
    )
    takes_skip = jnp.logical_or(
        jnp.where(odd == 0, seq < last, seq > 0), jnp.logical_or(me == 3, me == count - 4)
    )
    mate_skip = jnp.logical_or(inner, jnp.logical_or(me == 2, me == count - 3))
    gives_turn = jnp.where(high == 0, wrap_next, wrap_prev)
    flat_next = jnp.logical_and(has_next, seq % 4 != 3)
    flat_prev = jnp.logical_and(has_prev, seq % 4 != 0)
    gives_stream = jnp.where(high == 0, flat_prev, flat_next)
    takes_stream = jnp.where(high == 0, flat_next, flat_prev)
    mate_far = jnp.where(odd == 0, me + 1 < count - 1, me > 1)

    @pl.when(edge)
    def _():
        for ref in (far0, far1, x2, p2, px, x3, p3):
            ref[...] = jnp.zeros_like(ref)

    barrier = pltpu.get_barrier_semaphore()
    links = (
        (far_dev, has_far),
        (near_dev, None),
        (seq_prev, has_prev),
        (seq_next, has_next),
        (cross_dev, has_cross),
        (direct_dev, meets_own),
        (mirror_dev, jnp.logical_and(wraps, odd == high)),
    )
    for other, exists in links:
        when(exists, lambda: pl.semaphore_signal(
            barrier, inc=1, device_id=other, device_id_type=MESH
        ))

    row = lax.broadcasted_iota(jnp.int32, (BLK, BLK), 0)
    col = lax.broadcasted_iota(jnp.int32, (BLK, BLK), 1)
    perm[...] = jnp.where((row % SLAB) * 8 + row // SLAB == col, 1.0, 0.0).astype(BF)
    back[...] = jnp.where((col % SLAB) * 8 + col // SLAB == row, 1.0, 0.0).astype(BF)

    far_blk = odd
    near_blk = 1 - odd

    def columns(head):
        return pl.ds(pl.multiple_of(head * DIM, DIM), DIM)

    def halo0(side, kv, head):
        blk = (far_blk, near_blk)[side]
        return pltpu.make_async_remote_copy(
            src_ref=kv0.at[kv, pl.ds(pl.multiple_of(blk * BLK, BLK), BLK), columns(head)],
            dst_ref=(far0, near0)[side].at[head, kv],
            send_sem=halo0_send.at[side, kv, head],
            recv_sem=halo0_recv.at[side, kv, head],
            device_id=(far_dev, near_dev)[side],
            device_id_type=MESH,
        )

    def halo1(side, head):
        half = 1 - (far_blk, near_blk)[side]
        return pltpu.make_async_remote_copy(
            src_ref=kv1.at[head, half],
            dst_ref=(far1, near1)[side].at[head],
            send_sem=halo1_send.at[side, head],
            recv_sem=halo1_recv.at[side, head],
            device_id=(far_dev, near_dev)[side],
            device_id_type=MESH,
        )

    def n2_copy(leg, head):
        return pltpu.make_async_remote_copy(
            src_ref=n2.at[head],
            dst_ref=(p2, x2)[leg].at[head],
            send_sem=n2_send.at[leg, head],
            recv_sem=n2_recv.at[leg, head],
            device_id=(near_dev, skip_to)[leg],
            device_id_type=MESH,
        )

    def px_copy(head):
        return pltpu.make_async_remote_copy(
            src_ref=x2.at[head],
            dst_ref=px.at[head],
            send_sem=px_send.at[head],
            recv_sem=px_recv.at[head],
            device_id=near_dev,
            device_id_type=MESH,
        )

    stream_dev = spot(me - 4 + 8 * high)

    def c3_copy(head):
        return pltpu.make_async_remote_copy(
            src_ref=c3.at[head],
            dst_ref=x3.at[2, head],
            send_sem=c3_send.at[head],
            recv_sem=x3_recv.at[2, head],
            device_id=stream_dev,
            device_id_type=MESH,
        )

    def send_stream(head, part):
        @pl.when(gives_stream)
        def _():
            for kv in range(2):
                c3[head, kv] = fold(part[head, kv], (0.5, 1.0)[kv])
            c3_copy(head).start()

    def x3_copy(slot, head):
        return pltpu.make_async_remote_copy(
            src_ref=kv3.at[head],
            dst_ref=x3.at[slot, head],
            send_sem=x3_send.at[slot, head],
            recv_sem=x3_recv.at[slot, head],
            device_id=(seq_next, seq_prev, cross_dev)[slot],
            device_id_type=MESH,
        )

    def turn_copy(head):
        return pltpu.make_async_remote_copy(
            src_ref=x3.at[2, head],
            dst_ref=x3.at[1 - high, head],
            send_sem=turn_send.at[head],
            recv_sem=x3_recv.at[1 - high, head],
            device_id=mirror_dev,
            device_id_type=MESH,
        )

    def own_copy(head):
        return pltpu.make_async_remote_copy(
            src_ref=kv2.at[head],
            dst_ref=x2.at[head],
            send_sem=own_send.at[head],
            recv_sem=n2_recv.at[1, head],
            device_id=direct_dev,
            device_id_type=MESH,
        )

    def p3_copy(slot, head):
        return pltpu.make_async_remote_copy(
            src_ref=x3.at[slot, head],
            dst_ref=p3.at[slot, head],
            send_sem=p3_send.at[slot, head],
            recv_sem=p3_recv.at[slot, head],
            device_id=near_dev,
            device_id_type=MESH,
        )

    def out_copy(head):
        return pltpu.make_async_copy(out.at[head], o_hbm.at[:, columns(head)], out_sem.at[head])

    loads[0].wait()
    loads[1].wait()
    peers = sum(1 if exists is None else jnp.where(exists, 1, 0) for _, exists in links)
    pl.semaphore_wait(barrier, peers)

    @pl.when(has_far)
    def _():
        for head in range(2):
            for kv in range(2):
                halo0(0, kv, head).start()

    for head in range(2):
        for kv in range(2):
            halo0(1, kv, head).start()

    def pair_columns(pair):
        return pl.ds(pl.multiple_of(pair * 2 * DIM, 2 * DIM), 2 * DIM)

    def coarsen_pair(pair, carry):
        for kv in range(2):
            factor = (0.5, 1.0)[kv]
            for half in range(2):
                natural = kv0[kv, half * BLK : (half + 1) * BLK, pair_columns(pair)]
                slabs = jnp.dot(perm[...], natural, preferred_element_type=F32)
                first = fold(slabs, factor)
                second = fold(first, factor)
                third = fold(second, factor)
                for sub in range(2):
                    head = 2 * pair + sub
                    lanes = slice(sub * DIM, (sub + 1) * DIM)
                    kv1[head, half, kv] = first[:, lanes]
                    kv2[head, kv, half * 64 : (half + 1) * 64, :] = second[:, lanes]
                    kv3[head, kv, half * SLAB : (half + 1) * SLAB, :] = third[:, lanes]
        return carry

    lax.fori_loop(0, HEADS // 2, coarsen_pair, 0)

    third_to = (
        jnp.logical_and(has_next, jnp.logical_not(jnp.logical_and(wrap_next, high == 0))),
        jnp.logical_and(has_prev, jnp.logical_not(jnp.logical_and(wrap_prev, high == 1))),
        gives_turn,
    )
    third_from = (has_prev, has_next, has_cross)
    def send_side(side, head):
        for kv in range(2):
            halo0(side, kv, head).start()
        halo1(side, head).start()

    @pl.when(has_far)
    def _():
        halo1(0, 0).start()
        halo1(0, 1).start()
        lax.fori_loop(2, window, lambda head, c: (send_side(0, head), c)[1], 0)

    halo1(1, 0).start()
    halo1(1, 1).start()
    lax.fori_loop(2, HEADS, lambda head, c: (send_side(1, head), c)[1], 0)

    loads[2].wait()

    def query_pair(pair, carry):
        for half in range(2):
            natural = q0[half * BLK : (half + 1) * BLK, pair_columns(pair)]
            slabs = jnp.dot(perm[...], natural, preferred_element_type=F32)
            first = fold(slabs, 0.5)
            second = fold(first, 0.5)
            third = fold(second, 0.5)
            for sub in range(2):
                head = 2 * pair + sub
                lanes = slice(sub * DIM, (sub + 1) * DIM)
                qs[head, half * BLK : (half + 1) * BLK, :] = slabs[:, lanes].astype(BF)
                q1[head, half] = first[:, lanes]
                q2[head, half * 64 : (half + 1) * 64, :] = second[:, lanes]
                q3[head, half * SLAB : (half + 1) * SLAB, :] = third[:, lanes]
        return carry

    lax.fori_loop(0, HEADS // 2, query_pair, 0)

    def hidden(exists):
        return jnp.where(exists, 0.0, NEG)

    far_bias = hidden(has_far)
    x2_bias = hidden(takes_skip)
    p2_bias = hidden(mate_far)
    px_bias = hidden(mate_skip)
    third_bias = [hidden(exists) for exists in (has_prev, has_next, has_cross)]

    def half_rows(blk):
        return pl.ds(pl.multiple_of(blk * BLK, BLK), BLK)

    def fine_levels(head):
        sums = []
        for ref in (far0, near0):
            for kv in range(2):
                slabs = jnp.dot(perm[...], ref[head, kv], preferred_element_type=F32)
                sums.append(fold(slabs, (0.5, 1.0)[kv]))
        own = (kv0[0, :, columns(head)], kv0[1, :, columns(head)], None)
        far = (far0[head, 0], far0[head, 1], far_bias)
        near = (near0[head, 0], near0[head, 1], None)
        for blk, part in ((far_blk, far), (near_blk, near)):
            peak, both = attend(qs[head, half_rows(blk), :], (own, part), 1.0)
            acc[head, half_rows(blk), :] = both
            top[head, half_rows(blk), :] = peak
        far_rest = (far1[head, 0], far1[head, 1], far_bias)
        near_rest = (near1[head, 0], near1[head, 1], None)
        far_sums = (sums[0], sums[1], far_bias)
        near_sums = (sums[2], sums[3], None)
        for blk, part in ((far_blk, near_sums), (near_blk, far_sums)):
            peak, both = attend(q1[head, blk], (far_rest, near_rest, part), 2.0)
            acc1[head, blk] = both
            top1[head, blk] = peak

    def finish(head):
        for slot in range(3):
            when(third_from[slot], lambda: p3_copy(slot, head).wait_recv())
        keys = [ref[slot, head, 0] for slot in range(3) for ref in (x3, p3)]
        values = [ref[slot, head, 1] for slot in range(3) for ref in (x3, p3)]
        peak3, both3 = attend(
            q3[head],
            [
                (
                    jnp.concatenate(keys[2 * slot : 2 * slot + 2], axis=0),
                    jnp.concatenate(values[2 * slot : 2 * slot + 2], axis=0),
                    third_bias[slot],
                )
                for slot in range(3)
            ],
            8.0,
        )
        when(mate_skip, lambda: px_copy(head).wait_recv())
        when(mate_far, lambda: n2_copy(0, head).wait_recv())
        peak2, both2 = attend(
            q2[head],
            [
                (ref[head, 0], ref[head, 1], bias)
                for ref, bias in ((x2, x2_bias), (p2, p2_bias), (px, px_bias))
            ],
            4.0,
        )

        def join(peak_a, both_a, peak_b, both_b):
            peak = jnp.maximum(peak_a, peak_b)
            scale_a = jnp.exp2((peak_a - peak) * RATE)
            scale_b = jnp.exp2((peak_b - peak) * RATE)
            both = jnp.concatenate(
                [
                    both_a[:, :DIM] * scale_a + both_b[:, :DIM] * scale_b,
                    both_a[:, DIM:] * scale_a + both_b[:, DIM:] * scale_b,
                ],
                axis=1,
            )
            return peak, both

        peak2, both2 = join(peak2, both2, spread(peak3, 2), spread(both3, 2))
        for half in range(2):
            rows2 = slice(half * 64, (half + 1) * 64)
            peak1, both1 = join(
                top1[head, half],
                acc1[head, half],
                spread(peak2[rows2], 2),
                spread(both2[rows2], 2),
            )
            rows = slice(half * BLK, (half + 1) * BLK)
            _, both = join(
                top[head, rows, :], acc[head, rows, :], spread(peak1, 2), spread(both1, 2)
            )
            ratio = (both[:, :DIM] / both[:, DIM:]).astype(BF)
            out[head, rows, :] = jnp.dot(
                back[...], ratio, preferred_element_type=F32
            ).astype(BF)
        out_copy(head).start()

    def send_second(head):
        for kv in range(2):
            factor = (0.5, 1.0)[kv]
            slabs = jnp.dot(perm[...], far0[head, kv], preferred_element_type=F32)
            n2[head, kv, 0:64, :] = fold(fold(slabs, factor), factor)
            n2[head, kv, 64:128, :] = fold(far1[head, kv], factor)
        n2_copy(0, head).start()
        when(gives_skip, lambda: n2_copy(1, head).start())
        when(odd != high, lambda: send_stream(head, n2))

    def relay(head):
        n2_copy(1, head).wait_recv()
        px_copy(head).start()
        when(odd == high, lambda: send_stream(head, x2))

    def give_third(head):
        for slot in range(3):
            when(third_to[slot], lambda: x3_copy(slot, head).start())

    def turn(head):
        x3_copy(2, head).wait_recv()
        turn_copy(head).start()

    def stream(head):
        awaited = (has_prev, has_next, takes_stream)
        for slot in range(3):
            when(awaited[slot], lambda: x3_copy(slot, head).wait_recv())
            when(third_from[slot], lambda: p3_copy(slot, head).start())

    def during(step, lag, action, exists=None):
        inside = jnp.logical_and(step >= lag, step < HEADS + lag)
        when(
            inside if exists is None else jnp.logical_and(inside, exists),
            lambda: action(step - lag),
        )

    def take_far(head):
        halo0(0, 0, head).wait_recv()
        halo0(0, 1, head).wait_recv()
        halo1(0, head).wait_recv()
        when(head < HEADS - window, lambda: send_side(0, head + window))
        send_second(head)

    def take_near(head):
        halo0(1, 0, head).wait_recv()
        halo0(1, 1, head).wait_recv()
        halo1(1, head).wait_recv()
        fine_levels(head)

    def each_step(step, carry):
        during(step, 0, take_far, has_far)
        during(step, 0, lambda head: own_copy(head).start(), gives_own)
        during(step, 0, give_third)
        during(step, TURN_LAG, turn, gives_turn)
        during(step, RELAY_LAG, relay, takes_skip)
        during(step, STREAM_LAG, stream)
        during(step, 0, take_near)
        during(step, FINISH_LAG, finish)
        return carry

    lax.fori_loop(0, HEADS + FINISH_LAG, each_step, 0)

    def drain(head, carry):
        @pl.when(has_far)
        def _():
            for kv in range(2):
                halo0(0, kv, head).wait_send()
            halo1(0, head).wait_send()
            n2_copy(0, head).wait_send()

        for kv in range(2):
            halo0(1, kv, head).wait_send()
        halo1(1, head).wait_send()
        when(gives_skip, lambda: n2_copy(1, head).wait_send())
        when(gives_own, lambda: own_copy(head).wait_send())
        when(gives_stream, lambda: c3_copy(head).wait_send())
        when(gives_turn, lambda: turn_copy(head).wait_send())
        for slot in range(3):
            when(third_to[slot], lambda: x3_copy(slot, head).wait_send())
            when(third_from[slot], lambda: p3_copy(slot, head).wait_send())
        when(takes_skip, lambda: px_copy(head).wait_send())
        out_copy(head).wait()
        return carry

    lax.fori_loop(0, HEADS, drain, 0)


def solution(mesh):
    count = mesh.shape["seq"] * mesh.shape["grp"]

    def local(query_vecs, key_vecs, value_vecs):
        anywhere = pl.BlockSpec(memory_space=pl.ANY)
        dma = pltpu.SemaphoreType.DMA
        return pl.pallas_call(
            lambda *refs: kernel(count, *refs),
            out_shape=jax.ShapeDtypeStruct((ROWS, COLS), BF),
            in_specs=[anywhere] * 3,
            out_specs=anywhere,
            scratch_shapes=[
                pltpu.VMEM((ROWS, COLS), BF),
                pltpu.VMEM((2, ROWS, COLS), BF),
                pltpu.VMEM((HEADS, ROWS, DIM), BF),
                pltpu.VMEM((HEADS, 2, 128, DIM), BF),
                pltpu.VMEM((HEADS, 128, DIM), BF),
                pltpu.VMEM((HEADS, 64, DIM), BF),
                pltpu.VMEM((HEADS, 2, 2, 128, DIM), BF),
                pltpu.VMEM((HEADS, 2, 64, DIM), BF),
                pltpu.VMEM((BLK, BLK), BF),
                pltpu.VMEM((BLK, BLK), BF),
                pltpu.VMEM((HEADS, 2, BLK, DIM), BF),
                pltpu.VMEM((HEADS, 2, 128, DIM), BF),
                pltpu.VMEM((HEADS, 2, BLK, DIM), BF),
                pltpu.VMEM((HEADS, 2, 128, DIM), BF),
                pltpu.VMEM((HEADS, 2, 128, DIM), BF),
                pltpu.VMEM((HEADS, 2, 128, DIM), BF),
                pltpu.VMEM((HEADS, 2, 128, DIM), BF),
                pltpu.VMEM((HEADS, 2, 128, DIM), BF),
                pltpu.VMEM((HEADS, 2, 128, DIM), BF),
                pltpu.VMEM((HEADS, 2, 64, DIM), BF),
                pltpu.VMEM((3, HEADS, 2, 64, DIM), BF),
                pltpu.VMEM((3, HEADS, 2, 64, DIM), BF),
                pltpu.VMEM((HEADS, ROWS, 2 * DIM), F32),
                pltpu.VMEM((HEADS, ROWS, DIM), F32),
                pltpu.VMEM((HEADS, 2, 128, 2 * DIM), F32),
                pltpu.VMEM((HEADS, 2, 128, DIM), F32),
                pltpu.VMEM((HEADS, ROWS, DIM), BF),
                dma((3,)),
                dma((2, 2, HEADS)),
                dma((2, 2, HEADS)),
                dma((2, HEADS)),
                dma((2, HEADS)),
                dma((2, HEADS)),
                dma((2, HEADS)),
                dma((HEADS,)),
                dma((HEADS,)),
                dma((3, HEADS)),
                dma((3, HEADS)),
                dma((3, HEADS)),
                dma((3, HEADS)),
                dma((HEADS,)),
                dma((HEADS,)),
                dma((HEADS,)),
                dma((HEADS,)),
            ],
            compiler_params=pltpu.CompilerParams(
                collective_id=0, has_side_effects=True, vmem_limit_bytes=63 * 1024 * 1024
            ),
        )(query_vecs, key_vecs, value_vecs)

    spec = P(("seq", "grp"), None)
    return jax.shard_map(
        local, mesh=mesh, in_specs=(spec, spec, spec), out_specs=spec, check_vma=False
    )
```

```python
import math

import jax
import jax.numpy as jnp
from jax import lax
from jax.experimental import pallas as pl
from jax.experimental.pallas import tpu as pltpu
from jax.sharding import PartitionSpec as P

HEADS = 8
DIM = 128
BLK = 256
SLAB = 32
ROWS = 512
COLS = HEADS * DIM
NEG = -1e30
RELAY_LAG = 2
TURN_LAG = 1
STREAM_LAG = 3
FINISH_LAG = 4
DIAGONAL_WINDOW = 3
STRAIGHT_WINDOW = 5
RATE = math.log2(math.e) / math.sqrt(DIM)
MESH = pl.DeviceIdType.MESH
BF = jnp.bfloat16
F32 = jnp.float32


def fold(value, factor):
    rows, width = value.shape
    paired = value.astype(F32).reshape(rows // (2 * SLAB), 2, SLAB, width)
    summed = paired[:, 0] + paired[:, 1]
    return (summed * factor).reshape(rows // 2, width).astype(BF)


def spread(value, times):
    rows, width = value.shape
    wide = jnp.broadcast_to(
        value.reshape(rows // SLAB, 1, SLAB, width), (rows // SLAB, times, SLAB, width)
    )
    return wide.reshape(rows * times, width)


def attend(query, parts, weight):
    scores = []
    peak = None
    for keys, _, bias in parts:
        block = lax.dot_general(
            query, keys, (((1,), (1,)), ((), ())), preferred_element_type=F32
        )
        if bias is not None:
            block = block + bias
        scores.append(block)
        for start in range(0, block.shape[1], DIM):
            piece = block[:, start : start + DIM]
            peak = piece if peak is None else jnp.maximum(peak, piece)
    peak = jnp.max(peak, axis=1, keepdims=True)
    both = None
    for block, (_, values, _) in zip(scores, parts):
        probs = jnp.exp2((block - peak) * RATE).astype(BF)
        tail = jnp.full((values.shape[0], DIM), weight, BF)
        term = jnp.dot(
            probs, jnp.concatenate([values, tail], axis=1), preferred_element_type=F32
        )
        both = term if both is None else both + term
    return jnp.broadcast_to(peak, (peak.shape[0], DIM)), both


def when(condition, action):
    if condition is None:
        action()
    else:
        pl.when(condition)(action)


def kernel(
    count,
    q_hbm,
    k_hbm,
    v_hbm,
    o_hbm,
    q0,
    kv0,
    qs,
    q1,
    q2,
    q3,
    kv1,
    kv3,
    perm,
    back,
    far0,
    far1,
    near0,
    near1,
    kv2,
    n2,
    x2,
    p2,
    px,
    c3,
    hub,
    x3,
    p3,
    acc,
    top,
    acc1,
    top1,
    out,
    in_sem,
    halo0_send,
    halo0_recv,
    halo1_send,
    halo1_recv,
    n2_send,
    n2_recv,
    px_send,
    px_recv,
    x3_send,
    x3_recv,
    p3_send,
    p3_recv,
    out_sem,
    own_send,
    turn_send,
    c3_send,
    end_send,
    end_recv,
    hub_send,
):
    groups = count // 4
    seq = lax.axis_index("seq")
    grp = lax.axis_index("grp")
    me = seq * 4 + grp
    odd = grp % 2
    high = grp // 2

    def spot(index):
        wrapped = (index + count) % count
        return (wrapped // 4, wrapped % 4)

    far_dev = spot(me - 1 + 2 * odd)
    near_dev = spot(me + 1 - 2 * odd)
    skip_to = spot(me - 4 + 8 * odd)
    direct_dev = spot(me + 3 - 6 * odd)
    mirror_dev = (seq, 3 - grp)
    seq_prev = ((seq + groups - 1) % groups, grp)
    seq_next = ((seq + 1) % groups, grp)
    cross_dev = ((seq + groups + 1 - 2 * high) % groups, 3 - grp)

    loads = [
        pltpu.make_async_copy(k_hbm, kv0.at[0], in_sem.at[0]),
        pltpu.make_async_copy(v_hbm, kv0.at[1], in_sem.at[1]),
        pltpu.make_async_copy(q_hbm, q0, in_sem.at[2]),
    ]
    for load in loads:
        load.start()

    last = groups - 1
    edge = jnp.logical_or(seq == 0, seq == last)
    has_far = jnp.logical_and(me > 0, me < count - 1)
    window = jnp.where(odd == high, DIAGONAL_WINDOW, STRAIGHT_WINDOW)
    has_prev = seq > 0
    has_next = seq < last
    has_cross = jnp.where(high == 0, seq < last, seq > 0)
    wrap_next = jnp.logical_and(seq % 4 == 3, has_next)
    wrap_prev = jnp.logical_and(seq % 4 == 0, has_prev)
    wraps = jnp.logical_or(wrap_next, wrap_prev)
    turned = jnp.logical_or(
        jnp.logical_and(grp == 2, wrap_next), jnp.logical_and(grp == 1, wrap_prev)
    )
    at_end = jnp.logical_or(me == 0, me == count - 1)
    is_hub = jnp.logical_or(me == 15, me == count - 16)
    by_hub = jnp.logical_or(me == 3, me == count - 4)
    end_dev = spot(jnp.where(at_end, me + jnp.where(me == 0, 15, -15), me + jnp.where(me == 15, -15, 15)))
    hub_dev = spot(
        jnp.where(is_hub, me + jnp.where(me == 15, -12, 12), me + jnp.where(me == 3, 12, -12))
    )
    inner = jnp.where(odd == 0, seq > 0, seq < last)
    gives_skip = jnp.logical_and(
        inner,
        jnp.logical_not(
            jnp.logical_or(
                jnp.logical_and(grp == 2, wrap_prev), jnp.logical_and(grp == 1, wrap_next)
            )
        ),
    )
    takes_skip = jnp.logical_or(
        jnp.where(odd == 0, seq < last, seq > 0), jnp.logical_or(me == 3, me == count - 4)
    )
    mate_skip = jnp.logical_or(inner, jnp.logical_or(me == 2, me == count - 3))
    gives_turn = jnp.where(high == 0, wrap_next, wrap_prev)
    flat_next = jnp.logical_and(has_next, seq % 4 != 3)
    flat_prev = jnp.logical_and(has_prev, seq % 4 != 0)
    gives_stream = jnp.where(high == 0, flat_prev, flat_next)
    takes_stream = jnp.where(high == 0, flat_next, flat_prev)
    mate_far = jnp.where(odd == 0, me + 1 < count - 1, me > 1)

    @pl.when(edge)
    def _():
        for ref in (far0, far1, x2, p2, px, x3, p3):
            ref[...] = jnp.zeros_like(ref)

    barrier = pltpu.get_barrier_semaphore()
    links = (
        (far_dev, has_far),
        (near_dev, None),
        (seq_prev, has_prev),
        (seq_next, has_next),
        (cross_dev, has_cross),
        (direct_dev, turned),
        (end_dev, jnp.logical_or(at_end, is_hub)),
        (hub_dev, jnp.logical_or(is_hub, by_hub)),
        (mirror_dev, jnp.logical_and(wraps, odd == high)),
    )
    for other, exists in links:
        when(exists, lambda: pl.semaphore_signal(
            barrier, inc=1, device_id=other, device_id_type=MESH
        ))

    row = lax.broadcasted_iota(jnp.int32, (BLK, BLK), 0)
    col = lax.broadcasted_iota(jnp.int32, (BLK, BLK), 1)
    perm[...] = jnp.where((row % SLAB) * 8 + row // SLAB == col, 1.0, 0.0).astype(BF)
    back[...] = jnp.where((col % SLAB) * 8 + col // SLAB == row, 1.0, 0.0).astype(BF)

    far_blk = odd
    near_blk = 1 - odd

    def columns(head):
        return pl.ds(pl.multiple_of(head * DIM, DIM), DIM)

    def halo0(side, kv, head):
        blk = (far_blk, near_blk)[side]
        return pltpu.make_async_remote_copy(
            src_ref=kv0.at[kv, pl.ds(pl.multiple_of(blk * BLK, BLK), BLK), columns(head)],
            dst_ref=(far0, near0)[side].at[head, kv],
            send_sem=halo0_send.at[side, kv, head],
            recv_sem=halo0_recv.at[side, kv, head],
            device_id=(far_dev, near_dev)[side],
            device_id_type=MESH,
        )

    def halo1(side, head):
        half = 1 - (far_blk, near_blk)[side]
        return pltpu.make_async_remote_copy(
            src_ref=kv1.at[head, half],
            dst_ref=(far1, near1)[side].at[head],
            send_sem=halo1_send.at[side, head],
            recv_sem=halo1_recv.at[side, head],
            device_id=(far_dev, near_dev)[side],
            device_id_type=MESH,
        )

    def n2_copy(leg, head):
        return pltpu.make_async_remote_copy(
            src_ref=n2.at[head],
            dst_ref=(p2, x2)[leg].at[head],
            send_sem=n2_send.at[leg, head],
            recv_sem=n2_recv.at[leg, head],
            device_id=(near_dev, skip_to)[leg],
            device_id_type=MESH,
        )

    def px_copy(head):
        return pltpu.make_async_remote_copy(
            src_ref=x2.at[head],
            dst_ref=px.at[head],
            send_sem=px_send.at[head],
            recv_sem=px_recv.at[head],
            device_id=near_dev,
            device_id_type=MESH,
        )

    stream_dev = spot(me - 4 + 8 * high)

    def c3_copy(head):
        return pltpu.make_async_remote_copy(
            src_ref=c3.at[head],
            dst_ref=x3.at[2, head],
            send_sem=c3_send.at[head],
            recv_sem=x3_recv.at[2, head],
            device_id=stream_dev,
            device_id_type=MESH,
        )

    def send_stream(head, part):
        @pl.when(gives_stream)
        def _():
            for kv in range(2):
                c3[head, kv] = fold(part[head, kv], (0.5, 1.0)[kv])
            c3_copy(head).start()

    def x3_copy(slot, head):
        return pltpu.make_async_remote_copy(
            src_ref=kv3.at[head],
            dst_ref=x3.at[slot, head],
            send_sem=x3_send.at[slot, head],
            recv_sem=x3_recv.at[slot, head],
            device_id=(seq_next, seq_prev, cross_dev)[slot],
            device_id_type=MESH,
        )

    def turn_copy(head):
        return pltpu.make_async_remote_copy(
            src_ref=x3.at[2, head],
            dst_ref=x3.at[1 - high, head],
            send_sem=turn_send.at[head],
            recv_sem=x3_recv.at[1 - high, head],
            device_id=mirror_dev,
            device_id_type=MESH,
        )

    def own_copy(head):
        return pltpu.make_async_remote_copy(
            src_ref=kv2.at[head],
            dst_ref=x2.at[head],
            send_sem=own_send.at[head],
            recv_sem=n2_recv.at[1, head],
            device_id=direct_dev,
            device_id_type=MESH,
        )

    def end_copy(head):
        return pltpu.make_async_remote_copy(
            src_ref=kv2.at[head],
            dst_ref=hub.at[head],
            send_sem=end_send.at[head],
            recv_sem=end_recv.at[head],
            device_id=end_dev,
            device_id_type=MESH,
        )

    def hub_copy(head):
        return pltpu.make_async_remote_copy(
            src_ref=hub.at[head],
            dst_ref=x2.at[head],
            send_sem=hub_send.at[head],
            recv_sem=n2_recv.at[1, head],
            device_id=hub_dev,
            device_id_type=MESH,
        )

    def hand_on(head):
        end_copy(head).wait_recv()
        hub_copy(head).start()

    def p3_copy(slot, head):
        return pltpu.make_async_remote_copy(
            src_ref=x3.at[slot, head],
            dst_ref=p3.at[slot, head],
            send_sem=p3_send.at[slot, head],
            recv_sem=p3_recv.at[slot, head],
            device_id=near_dev,
            device_id_type=MESH,
        )

    def out_copy(head):
        return pltpu.make_async_copy(out.at[head], o_hbm.at[:, columns(head)], out_sem.at[head])

    loads[0].wait()
    loads[1].wait()
    peers = sum(1 if exists is None else jnp.where(exists, 1, 0) for _, exists in links)
    pl.semaphore_wait(barrier, peers)

    @pl.when(has_far)
    def _():
        for head in range(2):
            for kv in range(2):
                halo0(0, kv, head).start()

    for head in range(2):
        for kv in range(2):
            halo0(1, kv, head).start()

    def pair_columns(pair):
        return pl.ds(pl.multiple_of(pair * 2 * DIM, 2 * DIM), 2 * DIM)

    def coarsen_pair(pair, carry):
        for kv in range(2):
            factor = (0.5, 1.0)[kv]
            for half in range(2):
                natural = kv0[kv, half * BLK : (half + 1) * BLK, pair_columns(pair)]
                slabs = jnp.dot(perm[...], natural, preferred_element_type=F32)
                first = fold(slabs, factor)
                second = fold(first, factor)
                third = fold(second, factor)
                for sub in range(2):
                    head = 2 * pair + sub
                    lanes = slice(sub * DIM, (sub + 1) * DIM)
                    kv1[head, half, kv] = first[:, lanes]
                    kv2[head, kv, half * 64 : (half + 1) * 64, :] = second[:, lanes]
                    kv3[head, kv, half * SLAB : (half + 1) * SLAB, :] = third[:, lanes]
        return carry

    lax.fori_loop(0, HEADS // 2, coarsen_pair, 0)

    third_to = (
        jnp.logical_and(has_next, jnp.logical_not(jnp.logical_and(wrap_next, high == 0))),
        jnp.logical_and(has_prev, jnp.logical_not(jnp.logical_and(wrap_prev, high == 1))),
        gives_turn,
    )
    third_from = (has_prev, has_next, has_cross)
    def send_side(side, head):
        for kv in range(2):
            halo0(side, kv, head).start()
        halo1(side, head).start()

    @pl.when(has_far)
    def _():
        halo1(0, 0).start()
        halo1(0, 1).start()
        lax.fori_loop(2, window, lambda head, c: (send_side(0, head), c)[1], 0)

    halo1(1, 0).start()
    halo1(1, 1).start()
    lax.fori_loop(2, HEADS, lambda head, c: (send_side(1, head), c)[1], 0)

    loads[2].wait()

    def query_pair(pair, carry):
        for half in range(2):
            natural = q0[half * BLK : (half + 1) * BLK, pair_columns(pair)]
            slabs = jnp.dot(perm[...], natural, preferred_element_type=F32)
            first = fold(slabs, 0.5)
            second = fold(first, 0.5)
            third = fold(second, 0.5)
            for sub in range(2):
                head = 2 * pair + sub
                lanes = slice(sub * DIM, (sub + 1) * DIM)
                qs[head, half * BLK : (half + 1) * BLK, :] = slabs[:, lanes].astype(BF)
                q1[head, half] = first[:, lanes]
                q2[head, half * 64 : (half + 1) * 64, :] = second[:, lanes]
                q3[head, half * SLAB : (half + 1) * SLAB, :] = third[:, lanes]
        return carry

    lax.fori_loop(0, HEADS // 2, query_pair, 0)

    def hidden(exists):
        return jnp.where(exists, 0.0, NEG)

    far_bias = hidden(has_far)
    x2_bias = hidden(takes_skip)
    p2_bias = hidden(mate_far)
    px_bias = hidden(mate_skip)
    third_bias = [hidden(exists) for exists in (has_prev, has_next, has_cross)]

    def half_rows(blk):
        return pl.ds(pl.multiple_of(blk * BLK, BLK), BLK)

    def fine_levels(head):
        sums = []
        for ref in (far0, near0):
            for kv in range(2):
                slabs = jnp.dot(perm[...], ref[head, kv], preferred_element_type=F32)
                sums.append(fold(slabs, (0.5, 1.0)[kv]))
        own = (kv0[0, :, columns(head)], kv0[1, :, columns(head)], None)
        far = (far0[head, 0], far0[head, 1], far_bias)
        near = (near0[head, 0], near0[head, 1], None)
        for blk, part in ((far_blk, far), (near_blk, near)):
            peak, both = attend(qs[head, half_rows(blk), :], (own, part), 1.0)
            acc[head, half_rows(blk), :] = both
            top[head, half_rows(blk), :] = peak
        far_rest = (far1[head, 0], far1[head, 1], far_bias)
        near_rest = (near1[head, 0], near1[head, 1], None)
        far_sums = (sums[0], sums[1], far_bias)
        near_sums = (sums[2], sums[3], None)
        for blk, part in ((far_blk, near_sums), (near_blk, far_sums)):
            peak, both = attend(q1[head, blk], (far_rest, near_rest, part), 2.0)
            acc1[head, blk] = both
            top1[head, blk] = peak

    def finish(head):
        for slot in range(3):
            when(third_from[slot], lambda: p3_copy(slot, head).wait_recv())
        keys = [ref[slot, head, 0] for slot in range(3) for ref in (x3, p3)]
        values = [ref[slot, head, 1] for slot in range(3) for ref in (x3, p3)]
        peak3, both3 = attend(
            q3[head],
            [
                (
                    jnp.concatenate(keys[2 * slot : 2 * slot + 2], axis=0),
                    jnp.concatenate(values[2 * slot : 2 * slot + 2], axis=0),
                    third_bias[slot],
                )
                for slot in range(3)
            ],
            8.0,
        )
        when(mate_skip, lambda: px_copy(head).wait_recv())
        when(mate_far, lambda: n2_copy(0, head).wait_recv())
        peak2, both2 = attend(
            q2[head],
            [
                (ref[head, 0], ref[head, 1], bias)
                for ref, bias in ((x2, x2_bias), (p2, p2_bias), (px, px_bias))
            ],
            4.0,
        )

        def join(peak_a, both_a, peak_b, both_b):
            peak = jnp.maximum(peak_a, peak_b)
            scale_a = jnp.exp2((peak_a - peak) * RATE)
            scale_b = jnp.exp2((peak_b - peak) * RATE)
            both = jnp.concatenate(
                [
                    both_a[:, :DIM] * scale_a + both_b[:, :DIM] * scale_b,
                    both_a[:, DIM:] * scale_a + both_b[:, DIM:] * scale_b,
                ],
                axis=1,
            )
            return peak, both

        peak2, both2 = join(peak2, both2, spread(peak3, 2), spread(both3, 2))
        for half in range(2):
            rows2 = slice(half * 64, (half + 1) * 64)
            peak1, both1 = join(
                top1[head, half],
                acc1[head, half],
                spread(peak2[rows2], 2),
                spread(both2[rows2], 2),
            )
            rows = slice(half * BLK, (half + 1) * BLK)
            _, both = join(
                top[head, rows, :], acc[head, rows, :], spread(peak1, 2), spread(both1, 2)
            )
            ratio = (both[:, :DIM] / both[:, DIM:]).astype(BF)
            out[head, rows, :] = jnp.dot(
                back[...], ratio, preferred_element_type=F32
            ).astype(BF)
        out_copy(head).start()

    def send_second(head):
        for kv in range(2):
            factor = (0.5, 1.0)[kv]
            slabs = jnp.dot(perm[...], far0[head, kv], preferred_element_type=F32)
            n2[head, kv, 0:64, :] = fold(fold(slabs, factor), factor)
            n2[head, kv, 64:128, :] = fold(far1[head, kv], factor)
        n2_copy(0, head).start()
        when(gives_skip, lambda: n2_copy(1, head).start())
        when(odd != high, lambda: send_stream(head, n2))

    def relay(head):
        n2_copy(1, head).wait_recv()
        px_copy(head).start()
        when(odd == high, lambda: send_stream(head, x2))

    def give_third(head):
        for slot in range(3):
            when(third_to[slot], lambda: x3_copy(slot, head).start())

    def turn(head):
        x3_copy(2, head).wait_recv()
        turn_copy(head).start()

    def stream(head):
        awaited = (has_prev, has_next, takes_stream)
        for slot in range(3):
            when(awaited[slot], lambda: x3_copy(slot, head).wait_recv())
            when(third_from[slot], lambda: p3_copy(slot, head).start())

    def during(step, lag, action, exists=None):
        inside = jnp.logical_and(step >= lag, step < HEADS + lag)
        when(
            inside if exists is None else jnp.logical_and(inside, exists),
            lambda: action(step - lag),
        )

    def take_far(head):
        halo0(0, 0, head).wait_recv()
        halo0(0, 1, head).wait_recv()
        halo1(0, head).wait_recv()
        when(head < HEADS - window, lambda: send_side(0, head + window))
        send_second(head)

    def take_near(head):
        halo0(1, 0, head).wait_recv()
        halo0(1, 1, head).wait_recv()
        halo1(1, head).wait_recv()
        fine_levels(head)

    def each_step(step, carry):
        during(step, 0, take_far, has_far)
        during(step, 0, lambda head: own_copy(head).start(), turned)
        during(step, 0, lambda head: end_copy(head).start(), at_end)
        during(step, TURN_LAG, hand_on, is_hub)
        during(step, 0, give_third)
        during(step, TURN_LAG, turn, gives_turn)
        during(step, RELAY_LAG, relay, takes_skip)
        during(step, STREAM_LAG, stream)
        during(step, 0, take_near)
        during(step, FINISH_LAG, finish)
        return carry

    lax.fori_loop(0, HEADS + FINISH_LAG, each_step, 0)

    def drain(head, carry):
        @pl.when(has_far)
        def _():
            for kv in range(2):
                halo0(0, kv, head).wait_send()
            halo1(0, head).wait_send()
            n2_copy(0, head).wait_send()

        for kv in range(2):
            halo0(1, kv, head).wait_send()
        halo1(1, head).wait_send()
        when(gives_skip, lambda: n2_copy(1, head).wait_send())
        when(turned, lambda: own_copy(head).wait_send())
        when(at_end, lambda: end_copy(head).wait_send())
        when(is_hub, lambda: hub_copy(head).wait_send())
        when(gives_stream, lambda: c3_copy(head).wait_send())
        when(gives_turn, lambda: turn_copy(head).wait_send())
        for slot in range(3):
            when(third_to[slot], lambda: x3_copy(slot, head).wait_send())
            when(third_from[slot], lambda: p3_copy(slot, head).wait_send())
        when(takes_skip, lambda: px_copy(head).wait_send())
        out_copy(head).wait()
        return carry

    lax.fori_loop(0, HEADS, drain, 0)


def solution(mesh):
    count = mesh.shape["seq"] * mesh.shape["grp"]

    def local(query_vecs, key_vecs, value_vecs):
        anywhere = pl.BlockSpec(memory_space=pl.ANY)
        dma = pltpu.SemaphoreType.DMA
        return pl.pallas_call(
            lambda *refs: kernel(count, *refs),
            out_shape=jax.ShapeDtypeStruct((ROWS, COLS), BF),
            in_specs=[anywhere] * 3,
            out_specs=anywhere,
            scratch_shapes=[
                pltpu.VMEM((ROWS, COLS), BF),
                pltpu.VMEM((2, ROWS, COLS), BF),
                pltpu.VMEM((HEADS, ROWS, DIM), BF),
                pltpu.VMEM((HEADS, 2, 128, DIM), BF),
                pltpu.VMEM((HEADS, 128, DIM), BF),
                pltpu.VMEM((HEADS, 64, DIM), BF),
                pltpu.VMEM((HEADS, 2, 2, 128, DIM), BF),
                pltpu.VMEM((HEADS, 2, 64, DIM), BF),
                pltpu.VMEM((BLK, BLK), BF),
                pltpu.VMEM((BLK, BLK), BF),
                pltpu.VMEM((HEADS, 2, BLK, DIM), BF),
                pltpu.VMEM((HEADS, 2, 128, DIM), BF),
                pltpu.VMEM((HEADS, 2, BLK, DIM), BF),
                pltpu.VMEM((HEADS, 2, 128, DIM), BF),
                pltpu.VMEM((HEADS, 2, 128, DIM), BF),
                pltpu.VMEM((HEADS, 2, 128, DIM), BF),
                pltpu.VMEM((HEADS, 2, 128, DIM), BF),
                pltpu.VMEM((HEADS, 2, 128, DIM), BF),
                pltpu.VMEM((HEADS, 2, 128, DIM), BF),
                pltpu.VMEM((HEADS, 2, 64, DIM), BF),
                pltpu.VMEM((HEADS, 2, 128, DIM), BF),
                pltpu.VMEM((3, HEADS, 2, 64, DIM), BF),
                pltpu.VMEM((3, HEADS, 2, 64, DIM), BF),
                pltpu.VMEM((HEADS, ROWS, 2 * DIM), F32),
                pltpu.VMEM((HEADS, ROWS, DIM), F32),
                pltpu.VMEM((HEADS, 2, 128, 2 * DIM), F32),
                pltpu.VMEM((HEADS, 2, 128, DIM), F32),
                pltpu.VMEM((HEADS, ROWS, DIM), BF),
                dma((3,)),
                dma((2, 2, HEADS)),
                dma((2, 2, HEADS)),
                dma((2, HEADS)),
                dma((2, HEADS)),
                dma((2, HEADS)),
                dma((2, HEADS)),
                dma((HEADS,)),
                dma((HEADS,)),
                dma((3, HEADS)),
                dma((3, HEADS)),
                dma((3, HEADS)),
                dma((3, HEADS)),
                dma((HEADS,)),
                dma((HEADS,)),
                dma((HEADS,)),
                dma((HEADS,)),
                dma((HEADS,)),
                dma((HEADS,)),
                dma((HEADS,)),
            ],
            compiler_params=pltpu.CompilerParams(
                collective_id=0, has_side_effects=True, vmem_limit_bytes=63 * 1024 * 1024
            ),
        )(query_vecs, key_vecs, value_vecs)

    spec = P(("seq", "grp"), None)
    return jax.shard_map(
        local, mesh=mesh, in_specs=(spec, spec, spec), out_specs=spec, check_vma=False
    )
```

```python
import math

import jax
import jax.numpy as jnp
from jax import lax
from jax.experimental import pallas as pl
from jax.experimental.pallas import tpu as pltpu
from jax.sharding import PartitionSpec as P

HEADS = 8
DIM = 128
BLK = 256
SLAB = 32
ROWS = 512
COLS = HEADS * DIM
NEG = -1e30
RELAY_LAG = 2
TURN_LAG = 1
STREAM_LAG = 3
FINISH_LAG = 4
DIAGONAL_WINDOW = 3
STRAIGHT_WINDOW = 8
RATE = math.log2(math.e) / math.sqrt(DIM)
MESH = pl.DeviceIdType.MESH
BF = jnp.bfloat16
F32 = jnp.float32


def fold(value, factor):
    rows, width = value.shape
    paired = value.astype(F32).reshape(rows // (2 * SLAB), 2, SLAB, width)
    summed = paired[:, 0] + paired[:, 1]
    return (summed * factor).reshape(rows // 2, width).astype(BF)


def spread(value, times):
    rows, width = value.shape
    wide = jnp.broadcast_to(
        value.reshape(rows // SLAB, 1, SLAB, width), (rows // SLAB, times, SLAB, width)
    )
    return wide.reshape(rows * times, width)


def attend(query, parts, weight):
    scores = []
    peak = None
    for keys, _, bias in parts:
        block = lax.dot_general(
            query, keys, (((1,), (1,)), ((), ())), preferred_element_type=F32
        )
        if bias is not None:
            block = block + bias
        scores.append(block)
        for start in range(0, block.shape[1], DIM):
            piece = block[:, start : start + DIM]
            peak = piece if peak is None else jnp.maximum(peak, piece)
    peak = jnp.max(peak, axis=1, keepdims=True)
    both = None
    for block, (_, values, _) in zip(scores, parts):
        probs = jnp.exp2((block - peak) * RATE).astype(BF)
        tail = jnp.full((values.shape[0], DIM), weight, BF)
        term = jnp.dot(
            probs, jnp.concatenate([values, tail], axis=1), preferred_element_type=F32
        )
        both = term if both is None else both + term
    return jnp.broadcast_to(peak, (peak.shape[0], DIM)), both


def when(condition, action):
    if condition is None:
        action()
    else:
        pl.when(condition)(action)


def kernel(
    count,
    q_hbm,
    k_hbm,
    v_hbm,
    o_hbm,
    q0,
    kv0,
    qs,
    q1,
    q2,
    q3,
    kv1,
    kv3,
    perm,
    back,
    far0,
    far1,
    near0,
    near1,
    kv2,
    n2,
    x2,
    p2,
    px,
    c3,
    hub,
    x3,
    p3,
    acc,
    top,
    acc1,
    top1,
    out,
    in_sem,
    halo0_send,
    halo0_recv,
    halo1_send,
    halo1_recv,
    n2_send,
    n2_recv,
    px_send,
    px_recv,
    x3_send,
    x3_recv,
    p3_send,
    p3_recv,
    out_sem,
    own_send,
    turn_send,
    c3_send,
    end_send,
    end_recv,
    hub_send,
):
    groups = count // 4
    seq = lax.axis_index("seq")
    grp = lax.axis_index("grp")
    me = seq * 4 + grp
    odd = grp % 2
    high = grp // 2

    def spot(index):
        wrapped = (index + count) % count
        return (wrapped // 4, wrapped % 4)

    far_dev = spot(me - 1 + 2 * odd)
    near_dev = spot(me + 1 - 2 * odd)
    skip_to = spot(me - 4 + 8 * odd)
    direct_dev = spot(me + 3 - 6 * odd)
    mirror_dev = (seq, 3 - grp)
    seq_prev = ((seq + groups - 1) % groups, grp)
    seq_next = ((seq + 1) % groups, grp)
    cross_dev = ((seq + groups + 1 - 2 * high) % groups, 3 - grp)

    loads = [
        pltpu.make_async_copy(k_hbm, kv0.at[0], in_sem.at[0]),
        pltpu.make_async_copy(v_hbm, kv0.at[1], in_sem.at[1]),
        pltpu.make_async_copy(q_hbm, q0, in_sem.at[2]),
    ]
    for load in loads:
        load.start()

    last = groups - 1
    edge = jnp.logical_or(seq == 0, seq == last)
    has_far = jnp.logical_and(me > 0, me < count - 1)
    window = jnp.where(odd == high, DIAGONAL_WINDOW, STRAIGHT_WINDOW)
    has_prev = seq > 0
    has_next = seq < last
    has_cross = jnp.where(high == 0, seq < last, seq > 0)
    wrap_next = jnp.logical_and(seq % 4 == 3, has_next)
    wrap_prev = jnp.logical_and(seq % 4 == 0, has_prev)
    wraps = jnp.logical_or(wrap_next, wrap_prev)
    turned = jnp.logical_or(
        jnp.logical_and(grp == 2, wrap_next), jnp.logical_and(grp == 1, wrap_prev)
    )
    at_end = jnp.logical_or(me == 0, me == count - 1)
    is_hub = jnp.logical_or(me == 15, me == count - 16)
    by_hub = jnp.logical_or(me == 3, me == count - 4)
    end_dev = spot(jnp.where(at_end, me + jnp.where(me == 0, 15, -15), me + jnp.where(me == 15, -15, 15)))
    hub_dev = spot(
        jnp.where(is_hub, me + jnp.where(me == 15, -12, 12), me + jnp.where(me == 3, 12, -12))
    )
    inner = jnp.where(odd == 0, seq > 0, seq < last)
    gives_skip = jnp.logical_and(
        inner,
        jnp.logical_not(
            jnp.logical_or(
                jnp.logical_and(grp == 2, wrap_prev), jnp.logical_and(grp == 1, wrap_next)
            )
        ),
    )
    takes_skip = jnp.logical_or(
        jnp.where(odd == 0, seq < last, seq > 0), jnp.logical_or(me == 3, me == count - 4)
    )
    mate_skip = jnp.logical_or(inner, jnp.logical_or(me == 2, me == count - 3))
    gives_turn = jnp.where(high == 0, wrap_next, wrap_prev)
    flat_next = jnp.logical_and(has_next, seq % 4 != 3)
    flat_prev = jnp.logical_and(has_prev, seq % 4 != 0)
    gives_stream = jnp.where(high == 0, flat_prev, flat_next)
    takes_stream = jnp.where(high == 0, flat_next, flat_prev)
    mate_far = jnp.where(odd == 0, me + 1 < count - 1, me > 1)

    @pl.when(edge)
    def _():
        for ref in (far0, far1, x2, p2, px, x3, p3):
            ref[...] = jnp.zeros_like(ref)

    barrier = pltpu.get_barrier_semaphore()
    links = (
        (far_dev, has_far),
        (near_dev, None),
        (seq_prev, has_prev),
        (seq_next, has_next),
        (cross_dev, has_cross),
        (direct_dev, turned),
        (end_dev, jnp.logical_or(at_end, is_hub)),
        (hub_dev, jnp.logical_or(is_hub, by_hub)),
        (mirror_dev, jnp.logical_and(wraps, odd == high)),
    )
    for other, exists in links:
        when(exists, lambda: pl.semaphore_signal(
            barrier, inc=1, device_id=other, device_id_type=MESH
        ))

    row = lax.broadcasted_iota(jnp.int32, (BLK, BLK), 0)
    col = lax.broadcasted_iota(jnp.int32, (BLK, BLK), 1)
    perm[...] = jnp.where((row % SLAB) * 8 + row // SLAB == col, 1.0, 0.0).astype(BF)
    back[...] = jnp.where((col % SLAB) * 8 + col // SLAB == row, 1.0, 0.0).astype(BF)

    far_blk = odd
    near_blk = 1 - odd

    def columns(head):
        return pl.ds(pl.multiple_of(head * DIM, DIM), DIM)

    def halo0(side, kv, head):
        blk = (far_blk, near_blk)[side]
        return pltpu.make_async_remote_copy(
            src_ref=kv0.at[kv, pl.ds(pl.multiple_of(blk * BLK, BLK), BLK), columns(head)],
            dst_ref=(far0, near0)[side].at[head, kv],
            send_sem=halo0_send.at[side, kv, head],
            recv_sem=halo0_recv.at[side, kv, head],
            device_id=(far_dev, near_dev)[side],
            device_id_type=MESH,
        )

    def halo1(side, head):
        half = 1 - (far_blk, near_blk)[side]
        return pltpu.make_async_remote_copy(
            src_ref=kv1.at[head, half],
            dst_ref=(far1, near1)[side].at[head],
            send_sem=halo1_send.at[side, head],
            recv_sem=halo1_recv.at[side, head],
            device_id=(far_dev, near_dev)[side],
            device_id_type=MESH,
        )

    def n2_copy(leg, head):
        return pltpu.make_async_remote_copy(
            src_ref=n2.at[head],
            dst_ref=(p2, x2)[leg].at[head],
            send_sem=n2_send.at[leg, head],
            recv_sem=n2_recv.at[leg, head],
            device_id=(near_dev, skip_to)[leg],
            device_id_type=MESH,
        )

    def px_copy(head):
        return pltpu.make_async_remote_copy(
            src_ref=x2.at[head],
            dst_ref=px.at[head],
            send_sem=px_send.at[head],
            recv_sem=px_recv.at[head],
            device_id=near_dev,
            device_id_type=MESH,
        )

    stream_dev = spot(me - 4 + 8 * high)

    def c3_copy(head):
        return pltpu.make_async_remote_copy(
            src_ref=c3.at[head],
            dst_ref=x3.at[2, head],
            send_sem=c3_send.at[head],
            recv_sem=x3_recv.at[2, head],
            device_id=stream_dev,
            device_id_type=MESH,
        )

    def send_stream(head, part):
        @pl.when(gives_stream)
        def _():
            for kv in range(2):
                c3[head, kv] = fold(part[head, kv], (0.5, 1.0)[kv])
            c3_copy(head).start()

    def x3_copy(slot, head):
        return pltpu.make_async_remote_copy(
            src_ref=kv3.at[head],
            dst_ref=x3.at[slot, head],
            send_sem=x3_send.at[slot, head],
            recv_sem=x3_recv.at[slot, head],
            device_id=(seq_next, seq_prev, cross_dev)[slot],
            device_id_type=MESH,
        )

    def turn_copy(head):
        return pltpu.make_async_remote_copy(
            src_ref=x3.at[2, head],
            dst_ref=x3.at[1 - high, head],
            send_sem=turn_send.at[head],
            recv_sem=x3_recv.at[1 - high, head],
            device_id=mirror_dev,
            device_id_type=MESH,
        )

    def own_copy(head):
        return pltpu.make_async_remote_copy(
            src_ref=kv2.at[head],
            dst_ref=x2.at[head],
            send_sem=own_send.at[head],
            recv_sem=n2_recv.at[1, head],
            device_id=direct_dev,
            device_id_type=MESH,
        )

    def end_copy(head):
        return pltpu.make_async_remote_copy(
            src_ref=kv2.at[head],
            dst_ref=hub.at[head],
            send_sem=end_send.at[head],
            recv_sem=end_recv.at[head],
            device_id=end_dev,
            device_id_type=MESH,
        )

    def hub_copy(head):
        return pltpu.make_async_remote_copy(
            src_ref=hub.at[head],
            dst_ref=x2.at[head],
            send_sem=hub_send.at[head],
            recv_sem=n2_recv.at[1, head],
            device_id=hub_dev,
            device_id_type=MESH,
        )

    def hand_on(head):
        end_copy(head).wait_recv()
        hub_copy(head).start()

    def p3_copy(slot, head):
        return pltpu.make_async_remote_copy(
            src_ref=x3.at[slot, head],
            dst_ref=p3.at[slot, head],
            send_sem=p3_send.at[slot, head],
            recv_sem=p3_recv.at[slot, head],
            device_id=near_dev,
            device_id_type=MESH,
        )

    def out_copy(head):
        return pltpu.make_async_copy(out.at[head], o_hbm.at[:, columns(head)], out_sem.at[head])

    loads[0].wait()
    loads[1].wait()
    peers = sum(1 if exists is None else jnp.where(exists, 1, 0) for _, exists in links)
    pl.semaphore_wait(barrier, peers)

    @pl.when(has_far)
    def _():
        for head in range(2):
            for kv in range(2):
                halo0(0, kv, head).start()

    for head in range(2):
        for kv in range(2):
            halo0(1, kv, head).start()

    def pair_columns(pair):
        return pl.ds(pl.multiple_of(pair * 2 * DIM, 2 * DIM), 2 * DIM)

    def coarsen_pair(pair, carry):
        for kv in range(2):
            factor = (0.5, 1.0)[kv]
            for half in range(2):
                natural = kv0[kv, half * BLK : (half + 1) * BLK, pair_columns(pair)]
                slabs = jnp.dot(perm[...], natural, preferred_element_type=F32)
                first = fold(slabs, factor)
                second = fold(first, factor)
                third = fold(second, factor)
                for sub in range(2):
                    head = 2 * pair + sub
                    lanes = slice(sub * DIM, (sub + 1) * DIM)
                    kv1[head, half, kv] = first[:, lanes]
                    kv2[head, kv, half * 64 : (half + 1) * 64, :] = second[:, lanes]
                    kv3[head, kv, half * SLAB : (half + 1) * SLAB, :] = third[:, lanes]
        return carry

    lax.fori_loop(0, HEADS // 2, coarsen_pair, 0)

    third_to = (
        jnp.logical_and(has_next, jnp.logical_not(jnp.logical_and(wrap_next, high == 0))),
        jnp.logical_and(has_prev, jnp.logical_not(jnp.logical_and(wrap_prev, high == 1))),
        gives_turn,
    )
    third_from = (has_prev, has_next, has_cross)
    def send_side(side, head):
        for kv in range(2):
            halo0(side, kv, head).start()
        halo1(side, head).start()

    @pl.when(has_far)
    def _():
        halo1(0, 0).start()
        halo1(0, 1).start()
        lax.fori_loop(2, window, lambda head, c: (send_side(0, head), c)[1], 0)

    halo1(1, 0).start()
    halo1(1, 1).start()
    lax.fori_loop(2, HEADS, lambda head, c: (send_side(1, head), c)[1], 0)

    loads[2].wait()

    def query_pair(pair, carry):
        for half in range(2):
            natural = q0[half * BLK : (half + 1) * BLK, pair_columns(pair)]
            slabs = jnp.dot(perm[...], natural, preferred_element_type=F32)
            first = fold(slabs, 0.5)
            second = fold(first, 0.5)
            third = fold(second, 0.5)
            for sub in range(2):
                head = 2 * pair + sub
                lanes = slice(sub * DIM, (sub + 1) * DIM)
                qs[head, half * BLK : (half + 1) * BLK, :] = slabs[:, lanes].astype(BF)
                q1[head, half] = first[:, lanes]
                q2[head, half * 64 : (half + 1) * 64, :] = second[:, lanes]
                q3[head, half * SLAB : (half + 1) * SLAB, :] = third[:, lanes]
        return carry

    lax.fori_loop(0, HEADS // 2, query_pair, 0)

    def hidden(exists):
        return jnp.where(exists, 0.0, NEG)

    far_bias = hidden(has_far)
    x2_bias = hidden(takes_skip)
    p2_bias = hidden(mate_far)
    px_bias = hidden(mate_skip)
    third_bias = [hidden(exists) for exists in (has_prev, has_next, has_cross)]

    def half_rows(blk):
        return pl.ds(pl.multiple_of(blk * BLK, BLK), BLK)

    def fine_levels(head):
        sums = []
        for ref in (far0, near0):
            for kv in range(2):
                slabs = jnp.dot(perm[...], ref[head, kv], preferred_element_type=F32)
                sums.append(fold(slabs, (0.5, 1.0)[kv]))
        own = (kv0[0, :, columns(head)], kv0[1, :, columns(head)], None)
        far = (far0[head, 0], far0[head, 1], far_bias)
        near = (near0[head, 0], near0[head, 1], None)
        for blk, part in ((far_blk, far), (near_blk, near)):
            peak, both = attend(qs[head, half_rows(blk), :], (own, part), 1.0)
            acc[head, half_rows(blk), :] = both
            top[head, half_rows(blk), :] = peak
        far_rest = (far1[head, 0], far1[head, 1], far_bias)
        near_rest = (near1[head, 0], near1[head, 1], None)
        far_sums = (sums[0], sums[1], far_bias)
        near_sums = (sums[2], sums[3], None)
        for blk, part in ((far_blk, near_sums), (near_blk, far_sums)):
            peak, both = attend(q1[head, blk], (far_rest, near_rest, part), 2.0)
            acc1[head, blk] = both
            top1[head, blk] = peak

    def finish(head):
        for slot in range(3):
            when(third_from[slot], lambda: p3_copy(slot, head).wait_recv())
        keys = [ref[slot, head, 0] for slot in range(3) for ref in (x3, p3)]
        values = [ref[slot, head, 1] for slot in range(3) for ref in (x3, p3)]
        peak3, both3 = attend(
            q3[head],
            [
                (
                    jnp.concatenate(keys[2 * slot : 2 * slot + 2], axis=0),
                    jnp.concatenate(values[2 * slot : 2 * slot + 2], axis=0),
                    third_bias[slot],
                )
                for slot in range(3)
            ],
            8.0,
        )
        when(mate_skip, lambda: px_copy(head).wait_recv())
        when(mate_far, lambda: n2_copy(0, head).wait_recv())
        peak2, both2 = attend(
            q2[head],
            [
                (ref[head, 0], ref[head, 1], bias)
                for ref, bias in ((x2, x2_bias), (p2, p2_bias), (px, px_bias))
            ],
            4.0,
        )

        def join(peak_a, both_a, peak_b, both_b):
            peak = jnp.maximum(peak_a, peak_b)
            scale_a = jnp.exp2((peak_a - peak) * RATE)
            scale_b = jnp.exp2((peak_b - peak) * RATE)
            both = jnp.concatenate(
                [
                    both_a[:, :DIM] * scale_a + both_b[:, :DIM] * scale_b,
                    both_a[:, DIM:] * scale_a + both_b[:, DIM:] * scale_b,
                ],
                axis=1,
            )
            return peak, both

        peak2, both2 = join(peak2, both2, spread(peak3, 2), spread(both3, 2))
        for half in range(2):
            rows2 = slice(half * 64, (half + 1) * 64)
            peak1, both1 = join(
                top1[head, half],
                acc1[head, half],
                spread(peak2[rows2], 2),
                spread(both2[rows2], 2),
            )
            rows = slice(half * BLK, (half + 1) * BLK)
            _, both = join(
                top[head, rows, :], acc[head, rows, :], spread(peak1, 2), spread(both1, 2)
            )
            ratio = (both[:, :DIM] / both[:, DIM:]).astype(BF)
            out[head, rows, :] = jnp.dot(
                back[...], ratio, preferred_element_type=F32
            ).astype(BF)
        out_copy(head).start()

    def send_second(head):
        for kv in range(2):
            factor = (0.5, 1.0)[kv]
            slabs = jnp.dot(perm[...], far0[head, kv], preferred_element_type=F32)
            n2[head, kv, 0:64, :] = fold(fold(slabs, factor), factor)
            n2[head, kv, 64:128, :] = fold(far1[head, kv], factor)
        n2_copy(0, head).start()
        when(gives_skip, lambda: n2_copy(1, head).start())
        when(odd != high, lambda: send_stream(head, n2))

    def relay(head):
        n2_copy(1, head).wait_recv()
        px_copy(head).start()
        when(odd == high, lambda: send_stream(head, x2))

    def give_third(head):
        for slot in range(3):
            when(third_to[slot], lambda: x3_copy(slot, head).start())

    def turn(head):
        x3_copy(2, head).wait_recv()
        turn_copy(head).start()

    def stream(head):
        awaited = (has_prev, has_next, takes_stream)
        for slot in range(3):
            when(awaited[slot], lambda: x3_copy(slot, head).wait_recv())
            when(third_from[slot], lambda: p3_copy(slot, head).start())

    def during(step, lag, action, exists=None):
        inside = jnp.logical_and(step >= lag, step < HEADS + lag)
        when(
            inside if exists is None else jnp.logical_and(inside, exists),
            lambda: action(step - lag),
        )

    def take_far(head):
        halo0(0, 0, head).wait_recv()
        halo0(0, 1, head).wait_recv()
        halo1(0, head).wait_recv()
        when(head < HEADS - window, lambda: send_side(0, head + window))
        send_second(head)

    def take_near(head):
        halo0(1, 0, head).wait_recv()
        halo0(1, 1, head).wait_recv()
        halo1(1, head).wait_recv()
        fine_levels(head)

    def each_step(step, carry):
        during(step, 0, take_far, has_far)
        during(step, 0, lambda head: own_copy(head).start(), turned)
        during(step, 0, lambda head: end_copy(head).start(), at_end)
        during(step, TURN_LAG, hand_on, is_hub)
        during(step, 0, give_third)
        during(step, TURN_LAG, turn, gives_turn)
        during(step, RELAY_LAG, relay, takes_skip)
        during(step, STREAM_LAG, stream)
        during(step, 0, take_near)
        during(step, FINISH_LAG, finish)
        return carry

    lax.fori_loop(0, HEADS + FINISH_LAG, each_step, 0)

    def drain(head, carry):
        @pl.when(has_far)
        def _():
            for kv in range(2):
                halo0(0, kv, head).wait_send()
            halo1(0, head).wait_send()
            n2_copy(0, head).wait_send()

        for kv in range(2):
            halo0(1, kv, head).wait_send()
        halo1(1, head).wait_send()
        when(gives_skip, lambda: n2_copy(1, head).wait_send())
        when(turned, lambda: own_copy(head).wait_send())
        when(at_end, lambda: end_copy(head).wait_send())
        when(is_hub, lambda: hub_copy(head).wait_send())
        when(gives_stream, lambda: c3_copy(head).wait_send())
        when(gives_turn, lambda: turn_copy(head).wait_send())
        for slot in range(3):
            when(third_to[slot], lambda: x3_copy(slot, head).wait_send())
            when(third_from[slot], lambda: p3_copy(slot, head).wait_send())
        when(takes_skip, lambda: px_copy(head).wait_send())
        out_copy(head).wait()
        return carry

    lax.fori_loop(0, HEADS, drain, 0)


def solution(mesh):
    count = mesh.shape["seq"] * mesh.shape["grp"]

    def local(query_vecs, key_vecs, value_vecs):
        anywhere = pl.BlockSpec(memory_space=pl.ANY)
        dma = pltpu.SemaphoreType.DMA
        return pl.pallas_call(
            lambda *refs: kernel(count, *refs),
            out_shape=jax.ShapeDtypeStruct((ROWS, COLS), BF),
            in_specs=[anywhere] * 3,
            out_specs=anywhere,
            scratch_shapes=[
                pltpu.VMEM((ROWS, COLS), BF),
                pltpu.VMEM((2, ROWS, COLS), BF),
                pltpu.VMEM((HEADS, ROWS, DIM), BF),
                pltpu.VMEM((HEADS, 2, 128, DIM), BF),
                pltpu.VMEM((HEADS, 128, DIM), BF),
                pltpu.VMEM((HEADS, 64, DIM), BF),
                pltpu.VMEM((HEADS, 2, 2, 128, DIM), BF),
                pltpu.VMEM((HEADS, 2, 64, DIM), BF),
                pltpu.VMEM((BLK, BLK), BF),
                pltpu.VMEM((BLK, BLK), BF),
                pltpu.VMEM((HEADS, 2, BLK, DIM), BF),
                pltpu.VMEM((HEADS, 2, 128, DIM), BF),
                pltpu.VMEM((HEADS, 2, BLK, DIM), BF),
                pltpu.VMEM((HEADS, 2, 128, DIM), BF),
                pltpu.VMEM((HEADS, 2, 128, DIM), BF),
                pltpu.VMEM((HEADS, 2, 128, DIM), BF),
                pltpu.VMEM((HEADS, 2, 128, DIM), BF),
                pltpu.VMEM((HEADS, 2, 128, DIM), BF),
                pltpu.VMEM((HEADS, 2, 128, DIM), BF),
                pltpu.VMEM((HEADS, 2, 64, DIM), BF),
                pltpu.VMEM((HEADS, 2, 128, DIM), BF),
                pltpu.VMEM((3, HEADS, 2, 64, DIM), BF),
                pltpu.VMEM((3, HEADS, 2, 64, DIM), BF),
                pltpu.VMEM((HEADS, ROWS, 2 * DIM), F32),
                pltpu.VMEM((HEADS, ROWS, DIM), F32),
                pltpu.VMEM((HEADS, 2, 128, 2 * DIM), F32),
                pltpu.VMEM((HEADS, 2, 128, DIM), F32),
                pltpu.VMEM((HEADS, ROWS, DIM), BF),
                dma((3,)),
                dma((2, 2, HEADS)),
                dma((2, 2, HEADS)),
                dma((2, HEADS)),
                dma((2, HEADS)),
                dma((2, HEADS)),
                dma((2, HEADS)),
                dma((HEADS,)),
                dma((HEADS,)),
                dma((3, HEADS)),
                dma((3, HEADS)),
                dma((3, HEADS)),
                dma((3, HEADS)),
                dma((HEADS,)),
                dma((HEADS,)),
                dma((HEADS,)),
                dma((HEADS,)),
                dma((HEADS,)),
                dma((HEADS,)),
                dma((HEADS,)),
            ],
            compiler_params=pltpu.CompilerParams(
                collective_id=0, has_side_effects=True, vmem_limit_bytes=63 * 1024 * 1024
            ),
        )(query_vecs, key_vecs, value_vecs)

    spec = P(("seq", "grp"), None)
    return jax.shard_map(
        local, mesh=mesh, in_specs=(spec, spec, spec), out_specs=spec, check_vma=False
    )
```
